256 devices in a mesh: dp: 32 (over z, x), head: 8 (over y, core).
Axes of the slice: x: 4, y: 4, z: 8, core: 2. Of those that a mesh axis runs over, the one named last changes fastest.
Arguments:
- acts: bfloat16 [16384, 7168], P('dp', 'head'), may hold values from -18 to 18
- latent: bfloat16 [16384, 512], P('dp'), may hold values from -6 to 6
- kv_gain: bfloat16 [512], replicated, may hold values from 0.099609375 to 1.8984375
- up_weight: bfloat16 [64, 512, 256], P('head'), may hold values from -0.25 to 0.25
- kv_cot: bfloat16 [16384, 64, 256], P('dp', 'head'), may hold values from -1.5 to 1.5
- rope_grad: bfloat16 [16384, 64], P('dp'), may hold values from -6 to 6
Outputs:
- down_update: bfloat16 [7168, 576], P('head')
- up_update: bfloat16 [64, 512, 256], P('head')
- down_rms: float32 [], replicated
The draws below stay inside these ranges and needn't reach their ends.
All inputs are finite; a program needn't handle non-finite values.
Results may differ from the reference program's by a relative error of at most 0.029.
Values may be sent and summed in bfloat16 or wider, within the bound.
A program may use at most 64 MiB of HBM per device.

```python
import math
import jax
import jax.numpy as jnp
from jax import lax

D = 7168
HEADS = 64
LAT = 512
ROPE = 64
DH = 128
NS_STEPS = 5
TOKENS = 16384


def draw_acts(key, part):
    columns = jnp.arange(D).astype(jnp.float32) / (D - 1)
    scales = 0.3 * jnp.exp(columns * jnp.log(10.0))
    values = jnp.clip(jax.random.normal(key, (TOKENS, D), jnp.float32), -6.0, 6.0)
    return (values * scales[None, :]).astype(jnp.bfloat16)


def block_levels(stream_key, dims, shards, least, largest):
    def one(axis_at, blocks):
        steps = jax.random.uniform(jax.random.fold_in(jax.random.fold_in(stream_key, 6), axis_at), (blocks,), jnp.float32, least / len(shards), largest / len(shards))
        return jnp.repeat(jnp.exp(steps), dims[axis_at] // blocks).reshape((-1,) + (1,) * (len(dims) - axis_at - 1))

    loudness = one(*shards[0])
    for cut in shards[1:]:
        loudness = loudness * one(*cut)
    return loudness


def noise(stream_key, dims, deviation, reach, shards=(), dtype=jnp.bfloat16):
    factor_of = block_levels(stream_key, dims, shards, -0.22, 0.18) if shards else 1.0
    values = jax.random.normal(stream_key, dims, jnp.float32) * deviation * factor_of
    return jnp.minimum(jnp.maximum(values, -reach), reach).astype(dtype)


def setup_inputs(seed: int = 0) -> dict:
    splits = jax.random.split(jax.random.key(seed), 7)
    return {
        "acts": draw_acts(jax.random.fold_in(splits[6], 71), 0),
        "latent": noise(splits[1], (TOKENS, LAT), 1.0, 6.0, ((0, 32),)),
        "kv_gain": jnp.clip(1.0 + 0.18 * jax.random.normal(splits[2], (LAT,), jnp.float32), 0.099609375, 1.8984375).astype(jnp.bfloat16),
        "up_weight": noise(splits[3], (HEADS, LAT, 2 * DH), LAT ** -0.5, 0.25, ((0, 8),)),
        "kv_cot": noise(splits[4], (TOKENS, HEADS, 2 * DH), 0.25, 1.5, ((0, 32), (1, 8))),
        "rope_grad": noise(splits[5], (TOKENS, ROPE), 1.0, 6.0, ((0, 32),)),
    }


coef_a = 3.4445
coef_b = -4.775
coef_c = 2.0315
highest = lax.Precision.HIGHEST

def orthogonalize(start, scale):
    current = start.astype(jnp.float32)
    for step in range(NS_STEPS):
        gram = jnp.einsum('brk,brl->bkl', current, current, precision=highest)
        square = jnp.einsum('bkl,blm->bkm', gram, gram, precision=highest)
        mixer = coef_b * gram + coef_c * square
        result = coef_a * current + jnp.einsum('brk,bkl->brl', current, mixer, precision=highest)
        if step == NS_STEPS - 1:
            return (scale * result).astype(jnp.bfloat16)
        current = lax.optimization_barrier(result.astype(jnp.bfloat16)).astype(jnp.float32)

def reference(acts, latent, kv_gain, up_weight, kv_cot, rope_grad):
    lat32 = latent.astype(jnp.float32)
    gain32 = kv_gain.astype(jnp.float32)
    inv = lax.rsqrt(lax.optimization_barrier(jnp.mean(lat32 * lat32, axis=1, keepdims=True)) + 1e-06)
    normed = (lat32 * inv * gain32).astype(jnp.bfloat16)
    cot32 = kv_cot.astype(jnp.float32)
    latent_cot = jnp.einsum('thk,hlk->tl', cot32, up_weight.astype(jnp.float32), precision=highest)
    scaled = latent_cot * gain32
    grad_latent = inv * scaled - lat32 * inv ** 3 * lax.optimization_barrier(jnp.mean(lat32 * scaled, axis=1, keepdims=True))
    compressed = jnp.concatenate([grad_latent.astype(jnp.bfloat16), rope_grad], axis=1)
    down_grad = jnp.einsum('td,tc->dc', acts.astype(jnp.float32), compressed.astype(jnp.float32), precision=highest)
    up_grad = jnp.einsum('tl,thk->hlk', normed.astype(jnp.float32), cot32, precision=highest)
    down_total = jnp.sum(down_grad * down_grad)
    down_rms = jnp.sqrt(down_total / float(TOKENS * D * (LAT + ROPE)))
    down_start = (down_grad / (jnp.sqrt(down_total) + 1e-07)).astype(jnp.bfloat16)
    up_norms = jnp.sqrt(lax.optimization_barrier(jnp.sum(up_grad * up_grad, axis=(1, 2))))
    up_start = (up_grad / (up_norms[:, None, None] + 1e-07)).astype(jnp.bfloat16)
    down_update = orthogonalize(down_start[None], 0.2 * math.sqrt(max(D, LAT + ROPE)))[0]
    up_update = orthogonalize(up_start, 0.2 * math.sqrt(max(LAT, 2 * DH)))
    return (down_update, up_update, down_rms)
```

```python
import functools
import math

import jax
import jax.numpy as jnp
from jax import lax
from jax.experimental import pallas as pl
from jax.experimental.pallas import tpu as pltpu
from jax.sharding import PartitionSpec as P

MESH = pl.DeviceIdType.MESH
bf16 = jnp.bfloat16
f32 = jnp.float32

D = 7168
TOKENS = 16384
LAT = 512
ROPE = 64
COLS = LAT + ROPE
WIDE = 640
DH2 = 256
NX, NZ, NY, NC = 4, 8, 4, 2
TOK = 512
HALF = TOK // NC
QUART = HALF // NY
DLOC = 896
XROWS = DLOC // NX
ZROWS = 32
UROWS = LAT // NX

coef_a = 3.4445
coef_b = -4.775
coef_c = 2.0315

BLOCK_ROWS = [128, 128, 128, 128, 64]
PACK = []
at = 0
for bi in range(5):
    for bj in range(bi, 5):
        PACK.append((bi, bj, at, BLOCK_ROWS[bi]))
        at += BLOCK_ROWS[bi]
PACKED = at
GHALF = PACKED // NC
GQUART = GHALF // NY


def dot(a, b):
    return lax.dot_general(a, b, (((1,), (0,)), ((), ())), preferred_element_type=f32)


def dot_nt(a, b):
    return lax.dot_general(a, b, (((1,), (1,)), ((), ())), preferred_element_type=f32)


def split(value):
    high = value.astype(bf16)
    low = (value - high.astype(f32)).astype(bf16)
    return high, low


def dot3(a, b):
    return dot(a[0], b[0]) + dot(a[0], b[1]) + dot(a[1], b[0])


def eye(n):
    rows = lax.broadcasted_iota(jnp.int32, (n, n), 0)
    cols = lax.broadcasted_iota(jnp.int32, (n, n), 1)
    return rows == cols


def mixer_of(a_ref, parts, n):
    square = dot3(parts, parts)
    mixed = coef_b * a_ref[...] + coef_c * square
    return mixed + jnp.where(eye(n), coef_a, 0.0)


def newton_schulz(a_ref, q_ref, n):
    a = split(a_ref[...])
    m = mixer_of(a_ref, a, n)
    q_ref[...] = m
    m = split(m)
    a_ref[...] = dot3(split(dot3(a, m)), m)

    def body(_, carry):
        a = split(a_ref[...])
        m = split(mixer_of(a_ref, a, n))
        a_ref[...] = dot3(split(dot3(a, m)), m)
        q_ref[...] = dot3(split(q_ref[...]), m)
        return carry

    lax.fori_loop(0, 3, body, 0)
    m = split(mixer_of(a_ref, split(a_ref[...]), n))
    q_ref[...] = dot3(split(q_ref[...]), m)


def kernel(
    kv, w, acts, lat, gain, rope, down_out, up_out, rms_out,
    pcs, rcc, csum, ysend, yrecv, comp, acts_t, usend, uxr, uzs, uzr, u,
    dsend, dxr, zsend, zrecv, xrows, gpk, gcr, gsum, gyr, gfull, a_ref, q_ref, ua_ref, uq_ref,
    s_c, r_c, s_yr, r_yr, s_ya, r_ya, s_ca, r_ca,
    s_ux, r_ux, s_uz, r_uz, s_ua, r_ua, s_oz, r_oz, s_ox, r_ox,
    s_dx, r_dx, s_dz, r_dz, s_az, r_az, s_ax, r_ax,
    s_gc, r_gc, s_gr, r_gr, s_ga, r_ga, s_gb, r_gb,
):
    dp = lax.axis_index("dp")
    hd = lax.axis_index("head")
    z, x = dp // NX, dp % NX
    y, c = hd // NC, hd % NC

    def to_x(j):
        return (z * NX + (x + j) % NX, hd)

    def to_z(j):
        return (((z + j) % NZ) * NX + x, hd)

    def to_y(j):
        return (dp, ((y + j) % NY) * NC + c)

    other = (dp, y * NC + (1 - c))

    def send(src, dst, s, r, device):
        copy = pltpu.make_async_remote_copy(
            src_ref=src, dst_ref=dst, send_sem=s, recv_sem=r,
            device_id=device, device_id_type=MESH,
        )
        copy.start()
        return copy

    started = []

    def ds(start, size):
        return pl.ds(pl.multiple_of(start, size), size)

    barrier = pltpu.get_barrier_semaphore()
    peers = [other] + [to_y(j) for j in range(1, NY)]
    peers += [to_x(j) for j in range(1, NX)] + [to_z(j) for j in range(1, NZ)]
    for peer in peers:
        pl.semaphore_signal(barrier, inc=1, device_id=peer, device_id_type=MESH)

    def cot_rows(start):
        rows = ds(start, HALF)
        total = dot_nt(kv[rows, 0:DH2], w[0])
        for h in range(1, 8):
            total += dot_nt(kv[rows, h * DH2 : (h + 1) * DH2], w[h])
        return total

    pcs[...] = cot_rows((1 - c) * HALF).astype(bf16)
    pl.semaphore_wait(barrier, len(peers))
    first = send(pcs, rcc, s_c, r_c, other)
    started.append(first)
    csum[...] = cot_rows(c * HALF)
    first.wait_recv()
    csum[...] += rcc[...].astype(f32)
    ysend[...] = csum[...].astype(bf16)
    y_reduce = [
        send(ysend.at[ds(((y + j) % NY) * QUART, QUART)], yrecv.at[j - 1],
             s_yr.at[j - 1], r_yr.at[j - 1], to_y(j))
        for j in range(1, NY)
    ]
    started += y_reduce

    lat32 = lat[...].astype(f32)
    gain32 = gain[...].astype(f32)
    inv = lax.rsqrt(jnp.mean(lat32 * lat32, axis=1, keepdims=True) + 1e-06)
    normed_t = (lat32 * inv * gain32).T.astype(bf16)
    for h in range(8):
        cols = slice(h * DH2, (h + 1) * DH2)
        usend[:, cols] = dot(normed_t, kv[:, cols]).astype(bf16)
    u_x = [
        send(usend.at[ds(((x + j) % NX) * UROWS, UROWS)], uxr.at[j - 1],
             s_ux.at[j - 1], r_ux.at[j - 1], to_x(j))
        for j in range(1, NX)
    ]
    started += u_x

    total = csum[ds(y * QUART, QUART), :]
    for j in range(1, NY):
        y_reduce[j - 1].wait_recv()
        total += yrecv[j - 1].astype(f32)
    own = c * HALF + y * QUART
    lat_q = lat[ds(own, QUART), :].astype(f32)
    inv_q = lax.rsqrt(jnp.mean(lat_q * lat_q, axis=1, keepdims=True) + 1e-06)
    scaled = total * gain32
    grad = inv_q * scaled - lat_q * inv_q**3 * jnp.mean(lat_q * scaled, axis=1, keepdims=True)
    comp[ds(own, QUART), :] = grad.astype(bf16)
    mine = comp.at[ds(own, QUART)]
    y_all = [send(mine, mine, s_ya.at[j - 1], r_ya.at[j - 1], to_y(j)) for j in range(1, NY)]
    c_all = [send(mine, mine, s_ca.at[0], r_ca.at[0], other)]
    acts_t[...] = acts[...].T
    for j in range(1, NY):
        y_all[j - 1].wait_recv()
        piece = comp.at[ds(c * HALF + ((y - j + NY) % NY) * QUART, QUART)]
        c_all.append(send(piece, piece, s_ca.at[j], r_ca.at[j], other))
    started += y_all + c_all
    dsend[:, LAT:WIDE] = jnp.concatenate(
        [dot(acts_t[...], rope[...]).astype(bf16), jnp.zeros((DLOC, WIDE - COLS), bf16)], axis=1
    )
    for copy in c_all:
        copy.wait_recv()
    dsend[:, 0:LAT] = dot(acts_t[...], comp[...]).astype(bf16)
    d_x = [
        send(dsend.at[ds(((x + j) % NX) * XROWS, XROWS)], dxr.at[j - 1],
             s_dx.at[j - 1], r_dx.at[j - 1], to_x(j))
        for j in range(1, NX)
    ]
    started += d_x

    for copy in u_x:
        copy.wait_recv()
    for h in range(8):
        cols = slice(h * DH2, (h + 1) * DH2)
        part = usend[ds(x * UROWS, UROWS), cols].astype(f32)
        for j in range(NX - 1):
            part += uxr[j, :, cols].astype(f32)
        uzs[h] = part.astype(bf16)
    u_z = [
        send(uzs.at[(z + j) % NZ], uzr.at[j - 1], s_uz.at[j - 1], r_uz.at[j - 1], to_z(j))
        for j in range(1, NZ)
    ]
    started += u_z

    for copy in d_x:
        copy.wait_recv()
    part = dsend[ds(x * XROWS, XROWS), :].astype(f32)
    for j in range(NX - 1):
        part += dxr[j].astype(f32)
    zsend[0:XROWS, :] = part.astype(bf16)
    zsend[XROWS : NZ * ZROWS, :] = jnp.zeros((NZ * ZROWS - XROWS, WIDE), bf16)
    d_z = [
        send(zsend.at[ds(((z + j) % NZ) * ZROWS, ZROWS)], zrecv.at[j - 1],
             s_dz.at[j - 1], r_dz.at[j - 1], to_z(j))
        for j in range(1, NZ)
    ]
    started += d_z

    part = uzs[z].astype(f32)
    for j in range(1, NZ):
        u_z[j - 1].wait_recv()
        part += uzr[j - 1].astype(f32)
    u_mine = u.at[ds(x * UROWS, UROWS)]
    u[ds(x * UROWS, UROWS), :] = part.astype(bf16)
    u_all = [send(u_mine, u_mine, s_ua.at[j - 1], r_ua.at[j - 1], to_x(j)) for j in range(1, NX)]
    started += u_all

    part = zsend[ds(z * ZROWS, ZROWS), :].astype(f32)
    for j in range(1, NZ):
        d_z[j - 1].wait_recv()
        part += zrecv[j - 1].astype(f32)
    xrows[x, ds(z * ZROWS, ZROWS), :] = part.astype(bf16)
    z_mine = xrows.at[x, ds(z * ZROWS, ZROWS)]
    d_az = [send(z_mine, z_mine, s_az.at[j - 1], r_az.at[j - 1], to_z(j)) for j in range(1, NZ)]
    started += d_az

    for copy in u_all:
        copy.wait_recv()
    uval = u[...]
    ugram = dot(uval.astype(f32).T.astype(bf16), uval)
    usq = jnp.sum(jnp.where(eye(DH2), ugram, 0.0), keepdims=True)
    unorm = 1.0 / (jnp.sqrt(usq) + 1e-07)
    ua_ref[...] = ugram * unorm * unorm
    newton_schulz(ua_ref, uq_ref, DH2)

    for copy in d_az:
        copy.wait_recv()
    x_mine = xrows.at[x, pl.ds(0, XROWS)]
    d_ax = [send(x_mine, x_mine, s_ax.at[j - 1], r_ax.at[j - 1], to_x(j)) for j in range(1, NX)]
    started += d_ax

    uq = split(uq_ref[...] * (unorm * (0.2 * math.sqrt(LAT))))
    urow = u[ds(x * UROWS, UROWS), :]
    up_out[z, ds(x * UROWS, UROWS), :] = (dot(urow, uq[0]) + dot(urow, uq[1])).astype(bf16)
    o_mine = up_out.at[z, ds(x * UROWS, UROWS)]
    o_z = [send(o_mine, o_mine, s_oz.at[j - 1], r_oz.at[j - 1], to_z(j)) for j in range(1, NZ)]
    started += o_z

    for copy in d_ax:
        copy.wait_recv()
    rows_t = [xrows[i, 0:XROWS, :].astype(f32).T.astype(bf16) for i in range(NX)]
    for bi in range(5):
        size = BLOCK_ROWS[bi]
        row = sum(
            dot(rows_t[i][bi * 128 : bi * 128 + size, :], xrows[i, 0:XROWS, bi * 128 : WIDE])
            for i in range(NX)
        )
        for pi, pj, start, _ in PACK:
            if pi == bi:
                gpk[start : start + size, :] = row[:, (pj - bi) * 128 : (pj - bi + 1) * 128]
    g_c = send(gpk.at[ds((1 - c) * GHALF, GHALF)], gcr, s_gc, r_gc, other)
    started.append(g_c)
    g_c.wait_recv()
    gsum[...] = gpk[ds(c * GHALF, GHALF), :] + gcr[...]
    g_y = [
        send(gsum.at[ds(((y + j) % NY) * GQUART, GQUART)], gyr.at[j - 1],
             s_gr.at[j - 1], r_gr.at[j - 1], to_y(j))
        for j in range(1, NY)
    ]
    started += g_y

    for copy in o_z:
        copy.wait_recv()
    o_rows = up_out.at[:, ds(x * UROWS, UROWS)]
    o_x = [send(o_rows, o_rows, s_ox.at[j - 1], r_ox.at[j - 1], to_x(j)) for j in range(1, NX)]
    started += o_x

    part = gsum[ds(y * GQUART, GQUART), :]
    for j in range(1, NY):
        g_y[j - 1].wait_recv()
        part += gyr[j - 1]
    own = c * GHALF + y * GQUART
    gfull[ds(own, GQUART), :] = part
    g_mine = gfull.at[ds(own, GQUART)]
    g_all = [send(g_mine, g_mine, s_ga.at[j - 1], r_ga.at[j - 1], to_y(j)) for j in range(1, NY)]
    g_fwd = [send(g_mine, g_mine, s_gb.at[0], r_gb.at[0], other)]
    for j in range(1, NY):
        g_all[j - 1].wait_recv()
        piece = gfull.at[ds(c * GHALF + ((y - j + NY) % NY) * GQUART, GQUART)]
        g_fwd.append(send(piece, piece, s_gb.at[j], r_gb.at[j], other))
    started += g_all + g_fwd
    for copy in g_fwd:
        copy.wait_recv()

    sq = jnp.zeros((1, 1), f32)
    for bi, bj, start, size in PACK:
        if bi == bj:
            block = gfull[start : start + size, :]
            row_id = lax.broadcasted_iota(jnp.int32, block.shape, 0)
            col_id = lax.broadcasted_iota(jnp.int32, block.shape, 1)
            sq += jnp.sum(jnp.where(row_id == col_id, block, 0.0), keepdims=True)
    norm = 1.0 / (jnp.sqrt(sq) + 1e-07)
    for bi, bj, start, size in PACK:
        block = gfull[start : start + size, :] * norm * norm
        wide = BLOCK_ROWS[bj]
        a_ref[bi * 128 : bi * 128 + size, bj * 128 : bj * 128 + wide] = block[:, 0:wide]
        if bi != bj:
            a_ref[bj * 128 : bj * 128 + wide, bi * 128 : bi * 128 + size] = block.T[0:wide, :]
    rms_out[0] = jnp.sqrt(sq / float(TOKENS * D * COLS))[0, 0]
    newton_schulz(a_ref, q_ref, COLS)
    q = split(q_ref[...] * (norm * (0.2 * math.sqrt(D))))
    for i in range(NX):
        rows = xrows[i, 0:XROWS, 0:COLS]
        out = dot(rows, q[0]) + dot(rows, q[1])
        down_out[i * XROWS : (i + 1) * XROWS, :] = out.astype(bf16)
    for copy in o_x:
        copy.wait_recv()
    for copy in started:
        copy.wait_send()


def per_device(acts, latent, kv_gain, up_weight, kv_cot, rope_grad):
    vmem = pltpu.VMEM
    dma = lambda *n: pltpu.SemaphoreType.DMA(n)
    sems = lambda n: [dma(n), dma(n)]
    scratch = [
        vmem((HALF, LAT), bf16), vmem((HALF, LAT), bf16), vmem((HALF, LAT), f32),
        vmem((HALF, LAT), bf16), vmem((3, QUART, LAT), bf16), vmem((TOK, LAT), bf16),
        vmem((DLOC, TOK), bf16),
        vmem((LAT, 8 * DH2), bf16), vmem((3, UROWS, 8 * DH2), bf16), vmem((8, UROWS, DH2), bf16),
        vmem((7, UROWS, DH2), bf16), vmem((LAT, DH2), bf16),
        vmem((DLOC, WIDE), bf16), vmem((3, XROWS, WIDE), bf16), vmem((NZ * ZROWS, WIDE), bf16),
        vmem((7, ZROWS, WIDE), bf16), vmem((NX, NZ * ZROWS, WIDE), bf16),
        vmem((PACKED, 128), f32), vmem((GHALF, 128), f32), vmem((GHALF, 128), f32),
        vmem((3, GQUART, 128), f32), vmem((PACKED, 128), f32),
        vmem((COLS, COLS), f32), vmem((COLS, COLS), f32), vmem((DH2, DH2), f32), vmem((DH2, DH2), f32),
    ]
    one = pltpu.SemaphoreType.DMA
    scratch += [one, one] + sems(3) + sems(3) + sems(4)
    scratch += sems(3) + sems(7) + sems(3) + sems(7) + sems(3)
    scratch += sems(3) + sems(7) + sems(7) + sems(3)
    scratch += [one, one] + sems(3) + sems(3) + sems(4)
    in_vmem = pl.BlockSpec(memory_space=pltpu.VMEM)
    down, up, rms = pl.pallas_call(
        kernel,
        out_shape=(
            jax.ShapeDtypeStruct((DLOC, COLS), bf16),
            jax.ShapeDtypeStruct((8, LAT, DH2), bf16),
            jax.ShapeDtypeStruct((1,), f32),
        ),
        in_specs=[in_vmem] * 6,
        out_specs=(in_vmem, in_vmem, pl.BlockSpec(memory_space=pltpu.SMEM)),
        scratch_shapes=scratch,
        name="muon",
        compiler_params=pltpu.CompilerParams(
            collective_id=0, has_side_effects=True, vmem_limit_bytes=62 * 1024 * 1024
        ),
    )(kv_cot.reshape(TOK, 8 * DH2), up_weight, acts, latent, kv_gain.reshape(1, LAT), rope_grad)
    return down, up, rms.reshape(())


def solution(mesh):
    in_specs = (
        P("dp", "head"),
        P("dp", None),
        P(),
        P("head", None, None),
        P("dp", "head", None),
        P("dp", None),
    )
    out_specs = (P("head", None), P("head", None, None), P())
    return jax.shard_map(
        per_device, mesh=mesh, in_specs=in_specs, out_specs=out_specs, check_vma=False
    )
```

```python
import functools
import math

import jax
import jax.numpy as jnp
from jax import lax
from jax.experimental import pallas as pl
from jax.experimental.pallas import tpu as pltpu
from jax.sharding import PartitionSpec as P

MESH = pl.DeviceIdType.MESH
bf16 = jnp.bfloat16
f32 = jnp.float32

D = 7168
TOKENS = 16384
LAT = 512
ROPE = 64
COLS = LAT + ROPE
DH2 = 256
NX, NZ, NY, NC = 4, 8, 4, 2
TOK = 512
HALF = TOK // NC
QUART = HALF // NY
DLOC = 896
XROWS = DLOC // NX
ZROWS = 32
UROWS = LAT // NX

coef_a = 3.4445
coef_b = -4.775
coef_c = 2.0315

BLOCK_ROWS = [128, 128, 128, 128, 64]
PACK = []
at = 0
for bi in range(5):
    for bj in range(bi, 5):
        PACK.append((bi, bj, at, BLOCK_ROWS[bi]))
        at += BLOCK_ROWS[bi]
PACKED = at
GHALF = PACKED // NC
GQUART = GHALF // NY


def dot(a, b):
    return lax.dot_general(a, b, (((1,), (0,)), ((), ())), preferred_element_type=f32)


def dot_nt(a, b):
    return lax.dot_general(a, b, (((1,), (1,)), ((), ())), preferred_element_type=f32)


def split(value):
    high = value.astype(bf16)
    low = (value - high.astype(f32)).astype(bf16)
    return high, low


def eye(rows, cols):
    row_id = lax.broadcasted_iota(jnp.int32, (rows, cols), 0)
    col_id = lax.broadcasted_iota(jnp.int32, (rows, cols), 1)
    return row_id == col_id


class Small:
    def prepare(self, value):
        return split(value[0])

    def product(self, a, b):
        return (dot(a[0], b[0]) + dot(a[0], b[1]) + dot(a[1], b[0]),)

    def rough(self, a, b):
        return (dot(a[0], b[0]),)


class Large:
    def prepare(self, value):
        main, corner = value
        rest = jnp.concatenate([main[LAT:, :].T, corner], axis=0)
        return split(main), split(rest)

    def product(self, a, b):
        (main_h, main_l), (rest_h, rest_l) = a
        (cols_h, cols_l), (tail_h, tail_l) = b
        rest = jnp.concatenate([rest_h, rest_l, rest_h], axis=1)
        low_rows = jnp.concatenate([cols_h[LAT:], cols_h[LAT:], cols_l[LAT:]], axis=0)
        main = dot(main_h, cols_h[:LAT]) + dot(main_h, cols_l[:LAT]) + dot(main_l, cols_h[:LAT])
        main += dot(rest, low_rows)
        low_tail = jnp.concatenate([tail_h[LAT:], tail_h[LAT:], tail_l[LAT:]], axis=0)
        corner = dot(main_h[LAT:], tail_h[:LAT]) + dot(main_h[LAT:], tail_l[:LAT])
        corner += dot(main_l[LAT:], tail_h[:LAT]) + dot(rest[LAT:], low_tail)
        return main, corner

    def rough(self, a, b):
        main_h, rest_h = a[0][0], a[1][0]
        cols_h, tail_h = b[0][0], b[1][0]
        main = dot(main_h, cols_h[:LAT]) + dot(rest_h, cols_h[LAT:])
        corner = dot(main_h[LAT:], tail_h[:LAT]) + dot(rest_h[LAT:], tail_h[LAT:])
        return main, corner


class NewtonSchulz:
    def __init__(self, form, gram, mix):
        self.form, self.gram, self.mix = form, gram, mix

    def load(self, refs):
        return tuple(ref[...] for ref in refs)

    def store(self, refs, value):
        for ref, part in zip(refs, value):
            ref[...] = part

    def mixer(self, parts):
        square = self.form.product(parts, parts)
        out = []
        for ref, part in zip(self.gram, square):
            out.append(coef_b * ref[...] + coef_c * part + jnp.where(eye(*part.shape), coef_a, 0.0))
        return tuple(out)

    def advance(self, parts, mixed):
        half = self.form.prepare(self.form.product(parts, mixed))
        self.store(self.gram, self.form.product(half, mixed))

    def first(self):
        parts = self.form.prepare(self.load(self.gram))
        mixed = self.mixer(parts)
        self.store(self.mix, mixed)
        self.advance(parts, self.form.prepare(mixed))

    def middle(self, count):
        def body(_, carry):
            parts = self.form.prepare(self.load(self.gram))
            mixed = self.form.prepare(self.mixer(parts))
            self.advance(parts, mixed)
            mix = self.form.prepare(self.load(self.mix))
            self.store(self.mix, self.form.product(mix, mixed))
            return carry

        lax.fori_loop(0, count, body, 0)

    def last(self):
        parts = self.form.prepare(self.load(self.gram))
        mixed = self.form.prepare(self.mixer(parts))
        mix = self.form.prepare(self.load(self.mix))
        return self.form.rough(mix, mixed)


def kernel(
    kv, w, acts, lat, gain, rope, down_out, up_out, rms_out,
    pcs, rcc, csum, ysend, yrecv, comp, acts_t, usend, uxr, uzs, uzr, u,
    dsend, dxr, zsend, zrecv, zrows, xall, esend, exr, fsend, frecv, frows, eall,
    gpk, gcr, gsum, gyr, gfull, a_main, a_corner, q_main, q_corner, ua_ref, uq_ref,
    s_c, r_c, s_yr, r_yr, s_ya, r_ya, s_ca, r_ca,
    s_ux, r_ux, s_uz, r_uz, s_ua, r_ua, s_oz, r_oz, s_ow, r_ow, s_ox, r_ox,
    s_dx, r_dx, s_dz, r_dz, s_az, r_az, s_ax, r_ax,
    s_ex, r_ex, s_ez, r_ez, s_fz, r_fz, s_fx, r_fx,
    s_gc, r_gc, s_gr, r_gr, s_ga, r_ga, s_gb, r_gb,
):
    dp = lax.axis_index("dp")
    hd = lax.axis_index("head")
    z, x = dp // NX, dp % NX
    y, c = hd // NC, hd % NC

    def to_x(j):
        return (z * NX + (x + j) % NX, hd)

    def to_z(j):
        return (((z + j) % NZ) * NX + x, hd)

    def to_y(j):
        return (dp, ((y + j) % NY) * NC + c)

    other = (dp, y * NC + (1 - c))
    started = []

    def send(src, dst, s, r, device):
        copy = pltpu.make_async_remote_copy(
            src_ref=src, dst_ref=dst, send_sem=s, recv_sem=r,
            device_id=device, device_id_type=MESH,
        )
        copy.start()
        started.append(copy)
        return copy

    def ds(start, size):
        return pl.ds(pl.multiple_of(start, size), size)

    barrier = pltpu.get_barrier_semaphore()
    peers = [other] + [to_y(j) for j in range(1, NY)]
    peers += [to_x(j) for j in range(1, NX)] + [to_z(j) for j in range(1, NZ)]
    for peer in peers:
        pl.semaphore_signal(barrier, inc=1, device_id=peer, device_id_type=MESH)

    def scatter_x(src, dst, s, r):
        return [
            send(src.at[ds(((x + j) % NX) * XROWS, XROWS)], dst.at[j - 1], s.at[j - 1], r.at[j - 1], to_x(j))
            for j in range(1, NX)
        ]

    def sum_x(copies, src, dst):
        for copy in copies:
            copy.wait_recv()
        part = src[ds(x * XROWS, XROWS), :].astype(f32)
        for j in range(NX - 1):
            part += dst[j].astype(f32)
        return part

    def scatter_z(part, src, dst, s, r):
        src[0:XROWS, :] = part.astype(bf16)
        src[XROWS : NZ * ZROWS, :] = jnp.zeros((NZ * ZROWS - XROWS, src.shape[1]), bf16)
        return [
            send(src.at[ds(((z + j) % NZ) * ZROWS, ZROWS)], dst.at[j - 1], s.at[j - 1], r.at[j - 1], to_z(j))
            for j in range(1, NZ)
        ]

    def sum_z(copies, src, dst):
        part = src[ds(z * ZROWS, ZROWS), :].astype(f32)
        for j in range(1, NZ):
            copies[j - 1].wait_recv()
            part += dst[j - 1].astype(f32)
        return part

    def gather_z(part, rows, s, r):
        rows[ds(z * ZROWS, ZROWS), :] = part.astype(bf16)
        mine = rows.at[ds(z * ZROWS, ZROWS)]
        return [send(mine, mine, s.at[j - 1], r.at[j - 1], to_z(j)) for j in range(1, NZ)]

    def gather_x(copies, rows, every, s, r):
        for copy in copies:
            copy.wait_recv()
        block = ds(x * XROWS, XROWS)
        out = [
            send(rows.at[pl.ds(0, XROWS)], every.at[block], s.at[j - 1], r.at[j - 1], to_x(j))
            for j in range(1, NX)
        ]
        every[block, :] = rows[0:XROWS, :]
        return out

    def cot_rows(start):
        rows = ds(start, HALF)
        total = dot_nt(kv[rows, 0:DH2], w[0])
        for h in range(1, 8):
            total += dot_nt(kv[rows, h * DH2 : (h + 1) * DH2], w[h])
        return total

    pcs[...] = cot_rows((1 - c) * HALF).astype(bf16)
    pl.semaphore_wait(barrier, len(peers))
    first = send(pcs, rcc, s_c, r_c, other)
    csum[...] = cot_rows(c * HALF)
    acts_t[...] = acts[...].T
    esend[...] = jnp.concatenate(
        [dot_nt(acts_t[...], rope[...]).astype(bf16), jnp.zeros((DLOC, 128 - ROPE), bf16)], axis=1
    )
    e_x = scatter_x(esend, exr, s_ex, r_ex)
    first.wait_recv()
    csum[...] += rcc[...].astype(f32)
    ysend[...] = csum[...].astype(bf16)
    y_reduce = [
        send(ysend.at[ds(((y + j) % NY) * QUART, QUART)], yrecv.at[j - 1],
             s_yr.at[j - 1], r_yr.at[j - 1], to_y(j))
        for j in range(1, NY)
    ]
    lat32 = lat[...].astype(f32)
    gain32 = gain[...].astype(f32)
    inv = lax.rsqrt(jnp.mean(lat32 * lat32, axis=1, keepdims=True) + 1e-06)
    normed_t = (lat32 * inv * gain32).T.astype(bf16)
    for h in range(8):
        cols = slice(h * DH2, (h + 1) * DH2)
        usend[:, cols] = dot(normed_t, kv[:, cols]).astype(bf16)

    def up_x(j):
        return send(usend.at[ds(((x + j) % NX) * UROWS, UROWS)], uxr.at[j - 1],
                    s_ux.at[j - 1], r_ux.at[j - 1], to_x(j))

    u_x = [up_x(1), up_x(3)]
    e_z = scatter_z(sum_x(e_x, esend, exr), fsend, frecv, s_ez, r_ez)
    total = csum[ds(y * QUART, QUART), :]
    for j in range(1, NY):
        y_reduce[j - 1].wait_recv()
        total += yrecv[j - 1].astype(f32)
    own = c * HALF + y * QUART
    lat_q = lat[ds(own, QUART), :].astype(f32)
    inv_q = lax.rsqrt(jnp.mean(lat_q * lat_q, axis=1, keepdims=True) + 1e-06)
    scaled = total * gain32
    grad = inv_q * scaled - lat_q * inv_q**3 * jnp.mean(lat_q * scaled, axis=1, keepdims=True)
    comp[ds(own, QUART), :] = grad.astype(bf16)
    mine = comp.at[ds(own, QUART)]
    y_all = [send(mine, mine, s_ya.at[j - 1], r_ya.at[j - 1], to_y(j)) for j in range(1, NY)]
    c_all = [send(mine, mine, s_ca.at[0], r_ca.at[0], other)]
    e_az = gather_z(sum_z(e_z, fsend, frecv), frows, s_fz, r_fz)
    for j in range(1, NY):
        y_all[j - 1].wait_recv()
        piece = comp.at[ds(c * HALF + ((y - j + NY) % NY) * QUART, QUART)]
        c_all.append(send(piece, piece, s_ca.at[j], r_ca.at[j], other))
    for copy in c_all:
        copy.wait_recv()
    dsend[...] = dot(acts_t[...], comp[...]).astype(bf16)
    d_x = scatter_x(dsend, dxr, s_dx, r_dx)
    u_x.append(up_x(2))
    e_ax = gather_x(e_az, frows, eall, s_fx, r_fx)
    d_z = scatter_z(sum_x(d_x, dsend, dxr), zsend, zrecv, s_dz, r_dz)
    d_az = gather_z(sum_z(d_z, zsend, zrecv), zrows, s_az, r_az)
    for copy in u_x:
        copy.wait_recv()
    for h in range(8):
        cols = slice(h * DH2, (h + 1) * DH2)
        part = usend[ds(x * UROWS, UROWS), cols].astype(f32)
        for j in range(NX - 1):
            part += uxr[j, :, cols].astype(f32)
        uzs[h] = part.astype(bf16)
    d_ax = gather_x(d_az, zrows, xall, s_ax, r_ax)
    u_z = [
        send(uzs.at[(z + j) % NZ], uzr.at[j - 1], s_uz.at[j - 1], r_uz.at[j - 1], to_z(j))
        for j in range(1, NZ)
    ]
    for copy in d_ax + e_ax:
        copy.wait_recv()
    main_t = [xall[:, i * 128 : (i + 1) * 128].astype(f32).T.astype(bf16) for i in range(4)]
    tail_t = eall[...].astype(f32).T.astype(bf16)
    for bi in range(5):
        size = BLOCK_ROWS[bi]
        lhs = main_t[bi] if bi < 4 else tail_t[0:size, :]
        tail = dot(lhs, eall[...])
        main = dot(lhs, xall[:, bi * 128 : LAT]) if bi < 4 else None
        for pi, pj, start, _ in PACK:
            if pi == bi:
                gpk[start : start + size, :] = tail if pj == 4 else main[:, (pj - bi) * 128 : (pj - bi + 1) * 128]
    g_c = send(gpk.at[ds((1 - c) * GHALF, GHALF)], gcr, s_gc, r_gc, other)
    part = uzs[z].astype(f32)
    for j in range(1, NZ):
        u_z[j - 1].wait_recv()
        part += uzr[j - 1].astype(f32)
    u_mine = u.at[ds(x * UROWS, UROWS)]
    u[ds(x * UROWS, UROWS), :] = part.astype(bf16)
    u_all = [send(u_mine, u_mine, s_ua.at[j - 1], r_ua.at[j - 1], to_x(j)) for j in range(1, NX)]
    g_c.wait_recv()
    gsum[...] = gpk[ds(c * GHALF, GHALF), :] + gcr[...]
    g_y = [
        send(gsum.at[ds(((y + j) % NY) * GQUART, GQUART)], gyr.at[j - 1],
             s_gr.at[j - 1], r_gr.at[j - 1], to_y(j))
        for j in range(1, NY)
    ]
    for copy in u_all:
        copy.wait_recv()
    uval = u[...]
    ugram = dot(uval.astype(f32).T.astype(bf16), uval)
    usq = jnp.sum(jnp.where(eye(DH2, DH2), ugram, 0.0), keepdims=True)
    unorm = 1.0 / (jnp.sqrt(usq) + 1e-07)
    ua_ref[...] = ugram * unorm * unorm
    up_steps = NewtonSchulz(Small(), (ua_ref,), (uq_ref,))
    up_steps.first()
    part = gsum[ds(y * GQUART, GQUART), :]
    for j in range(1, NY):
        g_y[j - 1].wait_recv()
        part += gyr[j - 1]
    own = c * GHALF + y * GQUART
    gfull[ds(own, GQUART), :] = part
    g_mine = gfull.at[ds(own, GQUART)]
    g_all = [send(g_mine, g_mine, s_ga.at[j - 1], r_ga.at[j - 1], to_y(j)) for j in range(1, NY)]
    g_fwd = [send(g_mine, g_mine, s_gb.at[0], r_gb.at[0], other)]
    up_steps.middle(3)
    uq = (up_steps.last()[0] * (unorm * (0.2 * math.sqrt(LAT)))).astype(bf16)
    near, far = ds(x * UROWS, UROWS), ds(((x + 2) % NX) * UROWS, UROWS)
    up_out[z, near, :] = dot(u[near, :], uq).astype(bf16)
    up_out[z, far, :] = dot(u[far, :], uq).astype(bf16)
    o_near, o_far = up_out.at[z, near], up_out.at[z, far]
    o_z = [send(o_near, o_near, s_oz.at[j - 1], r_oz.at[j - 1], to_z(j)) for j in range(1, NZ)]
    o_w = [send(o_far, o_far, s_ow.at[j - 1], r_ow.at[j - 1], to_z(j)) for j in range(1, NZ)]
    for j in range(1, NY):
        g_all[j - 1].wait_recv()
        piece = gfull.at[ds(c * GHALF + ((y - j + NY) % NY) * GQUART, GQUART)]
        g_fwd.append(send(piece, piece, s_gb.at[j], r_gb.at[j], other))
    for copy in g_fwd:
        copy.wait_recv()
    sq = jnp.zeros((1, 1), f32)
    for bi, bj, start, size in PACK:
        if bi == bj:
            block = gfull[start : start + size, :]
            sq += jnp.sum(jnp.where(eye(size, 128), block, 0.0), keepdims=True)
    norm = 1.0 / (jnp.sqrt(sq) + 1e-07)
    rms_out[0] = jnp.sqrt(sq / float(TOKENS * D * COLS))[0, 0]
    for bi, bj, start, size in PACK:
        block = gfull[start : start + size, :] * norm * norm
        rows = slice(bi * 128, bi * 128 + size)
        if bj < 4:
            a_main[rows, bj * 128 : (bj + 1) * 128] = block
        elif bi == 4:
            a_corner[...] = block[:, 0:ROPE]
        if bi != bj:
            wide = BLOCK_ROWS[bj]
            a_main[bj * 128 : bj * 128 + wide, rows] = block.T[0:wide, :]
    steps = NewtonSchulz(Large(), (a_main, a_corner), (q_main, q_corner))
    steps.first()
    for copy in o_z:
        copy.wait_recv()
    o_rows = up_out.at[:, near]
    o_x = [send(o_rows, o_rows, s_ox.at[i], r_ox.at[i], to_x(j)) for i, j in enumerate((1, 3))]
    steps.middle(3)
    main, corner = steps.last()
    scale = norm * (0.2 * math.sqrt(D))
    main = (main * scale).astype(bf16)
    rest = main[LAT:, :]
    corner = (corner * scale).astype(bf16)
    down_out[0:LAT, :] = (dot_nt(main[0:LAT], xall[...]) + dot(main[LAT:].astype(f32).T.astype(bf16), tail_t[0:ROPE])).astype(bf16)
    down_out[LAT:, :] = (dot_nt(rest, xall[...]) + dot(corner, tail_t[0:ROPE])).astype(bf16)
    for copy in o_w + o_x:
        copy.wait_recv()
    for copy in started:
        copy.wait_send()


def per_device(acts, latent, kv_gain, up_weight, kv_cot, rope_grad):
    vmem = pltpu.VMEM
    one = pltpu.SemaphoreType.DMA
    sems = lambda n: [pltpu.SemaphoreType.DMA((n,)), pltpu.SemaphoreType.DMA((n,))]

    def rows_of(width):
        return [
            vmem((DLOC, width), bf16), vmem((3, XROWS, width), bf16), vmem((NZ * ZROWS, width), bf16),
            vmem((7, ZROWS, width), bf16), vmem((NZ * ZROWS, width), bf16), vmem((DLOC, width), bf16),
        ]

    scratch = [
        vmem((HALF, LAT), bf16), vmem((HALF, LAT), bf16), vmem((HALF, LAT), f32),
        vmem((HALF, LAT), bf16), vmem((3, QUART, LAT), bf16), vmem((TOK, LAT), bf16),
        vmem((DLOC, TOK), bf16),
        vmem((LAT, 8 * DH2), bf16), vmem((3, UROWS, 8 * DH2), bf16), vmem((8, UROWS, DH2), bf16),
        vmem((7, UROWS, DH2), bf16), vmem((LAT, DH2), bf16),
    ]
    scratch += rows_of(LAT) + rows_of(128)
    scratch += [
        vmem((PACKED, 128), f32), vmem((GHALF, 128), f32), vmem((GHALF, 128), f32),
        vmem((3, GQUART, 128), f32), vmem((PACKED, 128), f32),
        vmem((COLS, LAT), f32), vmem((ROPE, ROPE), f32), vmem((COLS, LAT), f32), vmem((ROPE, ROPE), f32),
        vmem((DH2, DH2), f32), vmem((DH2, DH2), f32),
    ]
    scratch += [one, one] + sems(3) + sems(3) + sems(4)
    scratch += sems(3) + sems(7) + sems(3) + sems(7) + sems(7) + sems(2)
    scratch += sems(3) + sems(7) + sems(7) + sems(3)
    scratch += sems(3) + sems(7) + sems(7) + sems(3)
    scratch += [one, one] + sems(3) + sems(3) + sems(4)
    in_vmem = pl.BlockSpec(memory_space=pltpu.VMEM)
    down, up, rms = pl.pallas_call(
        kernel,
        out_shape=(
            jax.ShapeDtypeStruct((COLS, DLOC), bf16),
            jax.ShapeDtypeStruct((8, LAT, DH2), bf16),
            jax.ShapeDtypeStruct((1,), f32),
        ),
        in_specs=[in_vmem] * 6,
        out_specs=(in_vmem, in_vmem, pl.BlockSpec(memory_space=pltpu.SMEM)),
        scratch_shapes=scratch,
        name="muon",
        compiler_params=pltpu.CompilerParams(
            collective_id=0, has_side_effects=True, vmem_limit_bytes=62 * 1024 * 1024
        ),
    )(kv_cot.reshape(TOK, 8 * DH2), up_weight, acts, latent, kv_gain.reshape(1, LAT), rope_grad.T)
    return down.T, up, rms.reshape(())


def solution(mesh):
    in_specs = (
        P("dp", "head"),
        P("dp", None),
        P(),
        P("head", None, None),
        P("dp", "head", None),
        P("dp", None),
    )
    out_specs = (P("head", None), P("head", None, None), P())
    return jax.shard_map(
        per_device, mesh=mesh, in_specs=in_specs, out_specs=out_specs, check_vma=False
    )
```

```python
import functools
import math

import jax
import jax.numpy as jnp
from jax import lax
from jax.experimental import pallas as pl
from jax.experimental.pallas import tpu as pltpu
from jax.sharding import PartitionSpec as P

MESH = pl.DeviceIdType.MESH
bf16 = jnp.bfloat16
f32 = jnp.float32

D = 7168
TOKENS = 16384
LAT = 512
ROPE = 64
COLS = LAT + ROPE
DH2 = 256
NX, NZ, NY, NC = 4, 8, 4, 2
TOK = 512
HALF = TOK // NC
QUART = HALF // NY
DLOC = 896
XROWS = DLOC // NX
ZROWS = 32
UROWS = LAT // NX
AROWS, BROWS = 512, 384
AX, AZ = AROWS // NX, AROWS // (NX * NZ)
BZ, BX = BROWS // NZ, 16
UA, UB = 384, 128
UAX, UBX = UA // NX, UB // NX

VMEM_LIMIT = 40 * 1024 * 1024

coef_a = 3.4445
coef_b = -4.775
coef_c = 2.0315

BLOCK_ROWS = [128, 128, 128, 128, 64]
PACK = []
at = 0
for bi in range(5):
    for bj in range(bi, 5):
        PACK.append((bi, bj, at, BLOCK_ROWS[bi]))
        at += BLOCK_ROWS[bi]
PACKED = at
GHALF = PACKED // NC
GQUART = GHALF // NY


def dot(a, b):
    return lax.dot_general(a, b, (((1,), (0,)), ((), ())), preferred_element_type=f32)


def dot_nt(a, b):
    return lax.dot_general(a, b, (((1,), (1,)), ((), ())), preferred_element_type=f32)


def split(value):
    high = value.astype(bf16)
    low = (value - high.astype(f32)).astype(bf16)
    return high, low


def eye(rows, cols):
    row_id = lax.broadcasted_iota(jnp.int32, (rows, cols), 0)
    col_id = lax.broadcasted_iota(jnp.int32, (rows, cols), 1)
    return row_id == col_id


class Small:
    def prepare(self, value):
        return split(value[0])

    def product(self, a, b):
        return (dot(a[0], b[0]) + dot(a[0], b[1]) + dot(a[1], b[0]),)

    def rough(self, a, b):
        return (dot(a[0], b[0]),)


class Large:
    def prepare(self, value):
        main, corner = value
        rest = jnp.concatenate([main[LAT:, :].T, corner], axis=0)
        return split(main), split(rest)

    def product(self, a, b):
        (main_h, main_l), (rest_h, rest_l) = a
        (cols_h, cols_l), (tail_h, tail_l) = b
        rest = jnp.concatenate([rest_h, rest_l, rest_h], axis=1)
        low_rows = jnp.concatenate([cols_h[LAT:], cols_h[LAT:], cols_l[LAT:]], axis=0)
        main = dot(main_h, cols_h[:LAT]) + dot(main_h, cols_l[:LAT]) + dot(main_l, cols_h[:LAT])
        main += dot(rest, low_rows)
        low_tail = jnp.concatenate([tail_h[LAT:], tail_h[LAT:], tail_l[LAT:]], axis=0)
        corner = dot(main_h[LAT:], tail_h[:LAT]) + dot(main_h[LAT:], tail_l[:LAT])
        corner += dot(main_l[LAT:], tail_h[:LAT]) + dot(rest[LAT:], low_tail)
        return main, corner

    def rough(self, a, b):
        main_h, rest_h = a[0][0], a[1][0]
        cols_h, tail_h = b[0][0], b[1][0]
        main = dot(main_h, cols_h[:LAT]) + dot(rest_h, cols_h[LAT:])
        corner = dot(main_h[LAT:], tail_h[:LAT]) + dot(rest_h[LAT:], tail_h[LAT:])
        return main, corner


class NewtonSchulz:
    def __init__(self, form, gram, mix):
        self.form, self.gram, self.mix = form, gram, mix

    def load(self, refs):
        return tuple(ref[...] for ref in refs)

    def store(self, refs, value):
        for ref, part in zip(refs, value):
            ref[...] = part

    def mixer(self, parts):
        square = self.form.product(parts, parts)
        out = []
        for ref, part in zip(self.gram, square):
            out.append(coef_b * ref[...] + coef_c * part + jnp.where(eye(*part.shape), coef_a, 0.0))
        return tuple(out)

    def advance(self, parts, mixed):
        half = self.form.prepare(self.form.product(parts, mixed))
        self.store(self.gram, self.form.product(half, mixed))

    def first(self):
        parts = self.form.prepare(self.load(self.gram))
        mixed = self.mixer(parts)
        self.store(self.mix, mixed)
        self.advance(parts, self.form.prepare(mixed))

    def middle(self, count):
        def body(_, carry):
            parts = self.form.prepare(self.load(self.gram))
            mixed = self.form.prepare(self.mixer(parts))
            self.advance(parts, mixed)
            mix = self.form.prepare(self.load(self.mix))
            self.store(self.mix, self.form.product(mix, mixed))
            return carry

        lax.fori_loop(0, count, body, 0)

    def last(self):
        parts = self.form.prepare(self.load(self.gram))
        mixed = self.form.prepare(self.mixer(parts))
        mix = self.form.prepare(self.load(self.mix))
        return self.form.rough(mix, mixed)


def kernel(
    kv, w, acts, lat, gain, rope, up_out, rms_out, xall, eall, qm_out, qc_out,
    pcs, rcc, csum, ysend, yrecv, comp, acts_t, usend, uxr, uzs, uzr, vzr, vxs, vxr, u,
    dsend, axr, azs, azr, bzr, bxs, bxr, brow, esend, exr, fsend, frecv, frows,
    gpk, gcr, gsum, gyr, gfull, a_main, a_corner, q_main, q_corner, ua_ref, uq_ref,
    s_c, r_c, s_yr, r_yr, s_ya, r_ya, s_ca, r_ca,
    s_ux, r_ux, s_uz, r_uz, s_vz, r_vz, s_vx, r_vx, s_ua, r_ua, s_ub, r_ub, s_oz, r_oz, s_ow, r_ow, s_ox, r_ox,
    s_ax, r_ax, s_az, r_az, s_bz, r_bz, s_bx, r_bx,
    s_gaz, r_gaz, s_gax, r_gax, s_gbx, r_gbx, s_gbz, r_gbz,
    s_ex, r_ex, s_ez, r_ez, s_fz, r_fz, s_fx, r_fx,
    s_gc, r_gc, s_gr, r_gr, s_ga, r_ga, s_gb, r_gb,
):
    dp = lax.axis_index("dp")
    hd = lax.axis_index("head")
    z, x = dp // NX, dp % NX
    y, c = hd // NC, hd % NC

    def to_x(j):
        return (z * NX + (x + j) % NX, hd)

    def to_z(j):
        return (((z + j) % NZ) * NX + x, hd)

    def to_y(j):
        return (dp, ((y + j) % NY) * NC + c)

    other = (dp, y * NC + (1 - c))
    started = []

    def send(src, dst, s, r, device):
        copy = pltpu.make_async_remote_copy(
            src_ref=src, dst_ref=dst, send_sem=s, recv_sem=r,
            device_id=device, device_id_type=MESH,
        )
        copy.start()
        started.append(copy)
        return copy

    def ds(start, size, unit=None):
        return pl.ds(pl.multiple_of(start, unit or size), size)

    def to_all_x(src, dst, s, r):
        return [send(src(j), dst(j), s.at[j - 1], r.at[j - 1], to_x(j)) for j in range(1, NX)]

    def to_all_z(src, dst, s, r):
        return [send(src(j), dst(j), s.at[j - 1], r.at[j - 1], to_z(j)) for j in range(1, NZ)]

    def received(copies, total, slots):
        for i, copy in enumerate(copies):
            copy.wait_recv()
            total += slots[i].astype(f32)
        return total

    barrier = pltpu.get_barrier_semaphore()
    peers = [other] + [to_y(j) for j in range(1, NY)]
    peers += [to_x(j) for j in range(1, NX)] + [to_z(j) for j in range(1, NZ)]
    for peer in peers:
        pl.semaphore_signal(barrier, inc=1, device_id=peer, device_id_type=MESH)

    def scatter_x(src, dst, s, r):
        return [
            send(src.at[ds(((x + j) % NX) * XROWS, XROWS)], dst.at[j - 1], s.at[j - 1], r.at[j - 1], to_x(j))
            for j in range(1, NX)
        ]

    def sum_x(copies, src, dst):
        for copy in copies:
            copy.wait_recv()
        part = src[ds(x * XROWS, XROWS), :].astype(f32)
        for j in range(NX - 1):
            part += dst[j].astype(f32)
        return part

    def scatter_z(part, src, dst, s, r):
        src[0:XROWS, :] = part.astype(bf16)
        src[XROWS : NZ * ZROWS, :] = jnp.zeros((NZ * ZROWS - XROWS, src.shape[1]), bf16)
        return [
            send(src.at[ds(((z + j) % NZ) * ZROWS, ZROWS)], dst.at[j - 1], s.at[j - 1], r.at[j - 1], to_z(j))
            for j in range(1, NZ)
        ]

    def sum_z(copies, src, dst):
        part = src[ds(z * ZROWS, ZROWS), :].astype(f32)
        for j in range(1, NZ):
            copies[j - 1].wait_recv()
            part += dst[j - 1].astype(f32)
        return part

    def gather_z(part, rows, s, r):
        rows[ds(z * ZROWS, ZROWS), :] = part.astype(bf16)
        mine = rows.at[ds(z * ZROWS, ZROWS)]
        return [send(mine, mine, s.at[j - 1], r.at[j - 1], to_z(j)) for j in range(1, NZ)]

    def gather_x(copies, rows, every, s, r):
        for copy in copies:
            copy.wait_recv()
        block = ds(x * XROWS, XROWS)
        out = [
            send(rows.at[pl.ds(0, XROWS)], every.at[block], s.at[j - 1], r.at[j - 1], to_x(j))
            for j in range(1, NX)
        ]
        every[block, :] = rows[0:XROWS, :]
        return out

    def cot_rows(start):
        rows = ds(start, HALF)
        total = dot_nt(kv[rows, 0:DH2], w[0])
        for h in range(1, 8):
            total += dot_nt(kv[rows, h * DH2 : (h + 1) * DH2], w[h])
        return total

    pcs[...] = cot_rows((1 - c) * HALF).astype(bf16)
    pl.semaphore_wait(barrier, len(peers))
    first = send(pcs, rcc, s_c, r_c, other)
    csum[...] = cot_rows(c * HALF)
    acts_t[...] = acts[...].T
    esend[...] = jnp.concatenate(
        [dot_nt(acts_t[...], rope[...]).astype(bf16), jnp.zeros((DLOC, 128 - ROPE), bf16)], axis=1
    )
    e_x = scatter_x(esend, exr, s_ex, r_ex)
    first.wait_recv()
    csum[...] += rcc[...].astype(f32)
    ysend[...] = csum[...].astype(bf16)
    y_reduce = [
        send(ysend.at[ds(((y + j) % NY) * QUART, QUART)], yrecv.at[j - 1],
             s_yr.at[j - 1], r_yr.at[j - 1], to_y(j))
        for j in range(1, NY)
    ]
    lat32 = lat[...].astype(f32)
    gain32 = gain[...].astype(f32).reshape(1, LAT)
    inv = lax.rsqrt(jnp.mean(lat32 * lat32, axis=1, keepdims=True) + 1e-06)
    normed_t = (lat32 * inv * gain32).T.astype(bf16)
    for h in range(8):
        cols = slice(h * DH2, (h + 1) * DH2)
        usend[:, cols] = dot(normed_t, kv[:, cols]).astype(bf16)

    u_x = to_all_x(lambda j: usend.at[ds(((x + j) % NX) * UAX, UAX)], lambda j: uxr.at[j - 1], s_ux, r_ux)
    v_z = to_all_z(
        lambda j: usend.at[pl.ds(UA, UB), ds(((z + j) % NZ) * DH2, DH2)], lambda j: vzr.at[j - 1], s_vz, r_vz
    )
    e_z = scatter_z(sum_x(e_x, esend, exr), fsend, frecv, s_ez, r_ez)
    total = csum[ds(y * QUART, QUART), :]
    for j in range(1, NY):
        y_reduce[j - 1].wait_recv()
        total += yrecv[j - 1].astype(f32)
    own = c * HALF + y * QUART
    lat_q = lat[ds(own, QUART), :].astype(f32)
    inv_q = lax.rsqrt(jnp.mean(lat_q * lat_q, axis=1, keepdims=True) + 1e-06)
    scaled = total * gain32
    grad = inv_q * scaled - lat_q * inv_q**3 * jnp.mean(lat_q * scaled, axis=1, keepdims=True)
    comp[ds(own, QUART), :] = grad.astype(bf16)
    mine = comp.at[ds(own, QUART)]
    y_all = [send(mine, mine, s_ya.at[j - 1], r_ya.at[j - 1], to_y(j)) for j in range(1, NY)]
    c_all = [send(mine, mine, s_ca.at[0], r_ca.at[0], other)]
    e_az = gather_z(sum_z(e_z, fsend, frecv), frows, s_fz, r_fz)
    for j in range(1, NY):
        y_all[j - 1].wait_recv()
        piece = comp.at[ds(c * HALF + ((y - j + NY) % NY) * QUART, QUART)]
        c_all.append(send(piece, piece, s_ca.at[j], r_ca.at[j], other))
    for copy in c_all:
        copy.wait_recv()
    dsend[AROWS:, :] = dot(acts_t[AROWS:, :], comp[...]).astype(bf16)
    b_z = to_all_z(
        lambda j: dsend.at[ds(AROWS + ((z + j) % NZ) * BZ, BZ, 16)], lambda j: bzr.at[j - 1], s_bz, r_bz
    )
    dsend[0:AROWS, :] = dot(acts_t[0:AROWS, :], comp[...]).astype(bf16)
    a_x = to_all_x(lambda j: dsend.at[ds(((x + j) % NX) * AX, AX)], lambda j: axr.at[j - 1], s_ax, r_ax)
    e_ax = gather_x(e_az, frows, eall, s_fx, r_fx)
    part = received(v_z, usend[UA:, ds(z * DH2, DH2)].astype(f32), vzr)
    vxs[...] = part.astype(bf16)
    v_x = to_all_x(lambda j: vxs.at[ds(((x + j) % NX) * UBX, UBX)], lambda j: vxr.at[j - 1], s_vx, r_vx)
    azs[...] = received(a_x, dsend[ds(x * AX, AX), :].astype(f32), axr).astype(bf16)
    a_z = to_all_z(lambda j: azs.at[ds(((z + j) % NZ) * AZ, AZ)], lambda j: azr.at[j - 1], s_az, r_az)
    part = received(b_z, dsend[ds(AROWS + z * BZ, BZ, 16), :].astype(f32), bzr)
    bxs[0:BZ, :] = part.astype(bf16)
    bxs[BZ:, :] = jnp.zeros((NX * BX - BZ, LAT), bf16)
    b_x = to_all_x(lambda j: bxs.at[ds(((x + j) % NX) * BX, BX)], lambda j: bxr.at[j - 1], s_bx, r_bx)
    own = ds(x * AX + z * AZ, AZ)
    xall[own, :] = received(a_z, azs[ds(z * AZ, AZ), :].astype(f32), azr).astype(bf16)
    mine = xall.at[own]
    g_az = to_all_z(lambda j: mine, lambda j: mine, s_gaz, r_gaz)
    own_b = ds(x * BX, BX)
    brow[own_b, :] = received(b_x, bxs[own_b, :].astype(f32), bxr).astype(bf16)
    mine_b = brow.at[own_b]
    g_bx = to_all_x(lambda j: mine_b, lambda j: mine_b, s_gbx, r_gbx)
    for copy in g_bx:
        copy.wait_recv()
    own_z = ds(AROWS + z * BZ, BZ, 16)
    xall[own_z, :] = brow[0:BZ, :]
    mine_z = xall.at[own_z]
    g_bz = to_all_z(lambda j: mine_z, lambda j: mine_z, s_gbz, r_gbz)
    for copy in g_az:
        copy.wait_recv()
    mine_x = xall.at[ds(x * AX, AX)]
    g_ax = to_all_x(lambda j: mine_x, lambda j: mine_x, s_gax, r_gax)
    for copy in u_x:
        copy.wait_recv()
    for h in range(8):
        cols = slice(h * DH2, (h + 1) * DH2)
        part = usend[ds(x * UAX, UAX), cols].astype(f32)
        for j in range(NX - 1):
            part += uxr[j, :, cols].astype(f32)
        uzs[h] = part.astype(bf16)
    u_z = to_all_z(lambda j: uzs.at[(z + j) % NZ], lambda j: uzr.at[j - 1], s_uz, r_uz)
    for copy in g_ax + g_bz + e_ax:
        copy.wait_recv()
    main_t = [xall[:, i * 128 : (i + 1) * 128].astype(f32).T.astype(bf16) for i in range(4)]
    tail_t = eall[...].astype(f32).T.astype(bf16)
    for bi in range(5):
        size = BLOCK_ROWS[bi]
        lhs = main_t[bi] if bi < 4 else tail_t[0:size, :]
        tail = dot(lhs, eall[...])
        main = dot(lhs, xall[:, bi * 128 : LAT]) if bi < 4 else None
        for pi, pj, start, _ in PACK:
            if pi == bi:
                gpk[start : start + size, :] = tail if pj == 4 else main[:, (pj - bi) * 128 : (pj - bi + 1) * 128]
    g_c = send(gpk.at[ds((1 - c) * GHALF, GHALF)], gcr, s_gc, r_gc, other)
    g_c.wait_recv()
    gsum[...] = gpk[ds(c * GHALF, GHALF), :] + gcr[...]
    g_y = [
        send(gsum.at[ds(((y + j) % NY) * GQUART, GQUART)], gyr.at[j - 1],
             s_gr.at[j - 1], r_gr.at[j - 1], to_y(j))
        for j in range(1, NY)
    ]
    rows_a, rows_b = ds(x * UAX, UAX), ds(UA + x * UBX, UBX)
    u[rows_b, :] = received(v_x, vxs[ds(x * UBX, UBX), :].astype(f32), vxr).astype(bf16)
    u_b = to_all_x(lambda j: u.at[rows_b], lambda j: u.at[rows_b], s_ub, r_ub)
    u[rows_a, :] = received(u_z, uzs[z].astype(f32), uzr).astype(bf16)
    u_a = to_all_x(lambda j: u.at[rows_a], lambda j: u.at[rows_a], s_ua, r_ua)
    for copy in u_a + u_b:
        copy.wait_recv()
    uval = u[...]
    ugram = dot(uval.astype(f32).T.astype(bf16), uval)
    usq = jnp.sum(jnp.where(eye(DH2, DH2), ugram, 0.0), keepdims=True)
    unorm = 1.0 / (jnp.sqrt(usq) + 1e-07)
    ua_ref[...] = ugram * unorm * unorm
    up_steps = NewtonSchulz(Small(), (ua_ref,), (uq_ref,))
    up_steps.first()
    part = gsum[ds(y * GQUART, GQUART), :]
    for j in range(1, NY):
        g_y[j - 1].wait_recv()
        part += gyr[j - 1]
    own = c * GHALF + y * GQUART
    gfull[ds(own, GQUART), :] = part
    g_mine = gfull.at[ds(own, GQUART)]
    g_all = [send(g_mine, g_mine, s_ga.at[j - 1], r_ga.at[j - 1], to_y(j)) for j in range(1, NY)]
    g_fwd = [send(g_mine, g_mine, s_gb.at[0], r_gb.at[0], other)]
    up_steps.middle(3)
    uq = (up_steps.last()[0] * (unorm * (0.2 * math.sqrt(LAT)))).astype(bf16)
    near, far = ds(x * UROWS, UROWS), ds(((x + 2) % NX) * UROWS, UROWS)
    up_out[z, near, :] = dot(u[near, :], uq).astype(bf16)
    up_out[z, far, :] = dot(u[far, :], uq).astype(bf16)
    o_near, o_far = up_out.at[z, near], up_out.at[z, far]
    o_z = [send(o_near, o_near, s_oz.at[j - 1], r_oz.at[j - 1], to_z(j)) for j in range(1, NZ)]
    o_w = [send(o_far, o_far, s_ow.at[j - 1], r_ow.at[j - 1], to_z(j)) for j in range(1, NZ)]
    for j in range(1, NY):
        g_all[j - 1].wait_recv()
        piece = gfull.at[ds(c * GHALF + ((y - j + NY) % NY) * GQUART, GQUART)]
        g_fwd.append(send(piece, piece, s_gb.at[j], r_gb.at[j], other))
    for copy in g_fwd:
        copy.wait_recv()
    sq = jnp.zeros((1, 1), f32)
    for bi, bj, start, size in PACK:
        if bi == bj:
            block = gfull[start : start + size, :]
            sq += jnp.sum(jnp.where(eye(size, 128), block, 0.0), keepdims=True)
    norm = 1.0 / (jnp.sqrt(sq) + 1e-07)
    rms_out[0] = jnp.sqrt(sq / float(TOKENS * D * COLS))[0, 0]
    for bi, bj, start, size in PACK:
        block = gfull[start : start + size, :] * norm * norm
        rows = slice(bi * 128, bi * 128 + size)
        if bj < 4:
            a_main[rows, bj * 128 : (bj + 1) * 128] = block
        elif bi == 4:
            a_corner[...] = block[:, 0:ROPE]
        if bi != bj:
            wide = BLOCK_ROWS[bj]
            a_main[bj * 128 : bj * 128 + wide, rows] = block.T[0:wide, :]
    steps = NewtonSchulz(Large(), (a_main, a_corner), (q_main, q_corner))
    steps.first()
    for copy in o_z:
        copy.wait_recv()
    o_rows = up_out.at[:, near]
    o_x = [send(o_rows, o_rows, s_ox.at[i], r_ox.at[i], to_x(j)) for i, j in enumerate((1, 3))]
    steps.middle(3)
    main, corner = steps.last()
    scale = norm * (0.2 * math.sqrt(D))
    qm_out[...] = (main * scale).astype(bf16)
    qc_out[...] = (corner * scale).astype(bf16)
    for copy in o_w + o_x:
        copy.wait_recv()
    for copy in started:
        copy.wait_send()


def finish(qm, qc, xall, eall, up, down_out, up_out, sem):
    store = pltpu.make_async_copy(up, up_out, sem)
    store.start()
    tail = eall[:, 0:ROPE]
    side = qm[LAT:, :].astype(f32).T.astype(bf16)
    down_out[0:LAT, :] = (dot_nt(qm[0:LAT, :], xall[...]) + dot_nt(side, tail)).astype(bf16)
    down_out[LAT:, :] = (dot_nt(qm[LAT:, :], xall[...]) + dot_nt(qc[...], tail)).astype(bf16)
    store.wait()


def per_device(acts, latent, kv_gain, up_weight, kv_cot, rope_grad):
    vmem = pltpu.VMEM
    one = pltpu.SemaphoreType.DMA
    sems = lambda n: [pltpu.SemaphoreType.DMA((n,)), pltpu.SemaphoreType.DMA((n,))]

    scratch = [
        vmem((HALF, LAT), bf16), vmem((HALF, LAT), bf16), vmem((HALF, LAT), f32),
        vmem((HALF, LAT), bf16), vmem((3, QUART, LAT), bf16), vmem((TOK, LAT), bf16),
        vmem((DLOC, TOK), bf16),
        vmem((LAT, 8 * DH2), bf16), vmem((3, UAX, 8 * DH2), bf16), vmem((8, UAX, DH2), bf16),
        vmem((7, UAX, DH2), bf16), vmem((7, UB, DH2), bf16), vmem((UB, DH2), bf16),
        vmem((3, UBX, DH2), bf16), vmem((LAT, DH2), bf16),
        vmem((DLOC, LAT), bf16), vmem((3, AX, LAT), bf16), vmem((AX, LAT), bf16), vmem((7, AZ, LAT), bf16),
        vmem((7, BZ, LAT), bf16), vmem((NX * BX, LAT), bf16), vmem((3, BX, LAT), bf16),
        vmem((NX * BX, LAT), bf16),
        vmem((DLOC, 128), bf16), vmem((3, XROWS, 128), bf16), vmem((NZ * ZROWS, 128), bf16),
        vmem((7, ZROWS, 128), bf16), vmem((NZ * ZROWS, 128), bf16),
        vmem((PACKED, 128), f32), vmem((GHALF, 128), f32), vmem((GHALF, 128), f32),
        vmem((3, GQUART, 128), f32), vmem((PACKED, 128), f32),
        vmem((COLS, LAT), f32), vmem((ROPE, ROPE), f32), vmem((COLS, LAT), f32), vmem((ROPE, ROPE), f32),
        vmem((DH2, DH2), f32), vmem((DH2, DH2), f32),
    ]
    scratch += [one, one] + sems(3) + sems(3) + sems(4)
    scratch += sems(3) + sems(7) + sems(7) + sems(3) + sems(3) + sems(3) + sems(7) + sems(7) + sems(2)
    scratch += sems(3) + sems(7) + sems(7) + sems(3) + sems(7) + sems(3) + sems(3) + sems(7)
    scratch += sems(3) + sems(7) + sems(7) + sems(3)
    scratch += [one, one] + sems(3) + sems(3) + sems(4)
    in_vmem = pl.BlockSpec(memory_space=pltpu.VMEM)
    shape = jax.ShapeDtypeStruct
    up, rms, xall, eall, qm, qc = pl.pallas_call(
        kernel,
        out_shape=(
            shape((8, LAT, DH2), bf16), shape((1,), f32), shape((DLOC, LAT), bf16), shape((DLOC, 128), bf16),
            shape((COLS, LAT), bf16), shape((ROPE, ROPE), bf16),
        ),
        in_specs=[in_vmem] * 6,
        out_specs=(in_vmem, pl.BlockSpec(memory_space=pltpu.SMEM), in_vmem, in_vmem, in_vmem, in_vmem),
        scratch_shapes=scratch,
        name="muon",
        compiler_params=pltpu.CompilerParams(
            collective_id=0, has_side_effects=True, vmem_limit_bytes=VMEM_LIMIT
        ),
    )(kv_cot.reshape(TOK, 8 * DH2), up_weight, acts, latent, kv_gain, rope_grad.T)
    down, up = pl.pallas_call(
        finish,
        out_shape=(shape((COLS, DLOC), bf16), shape((8, LAT, DH2), bf16)),
        in_specs=[in_vmem] * 5,
        out_specs=(in_vmem, pl.BlockSpec(memory_space=pl.ANY)),
        scratch_shapes=[one],
        name="finish",
        compiler_params=pltpu.CompilerParams(vmem_limit_bytes=VMEM_LIMIT),
    )(qm, qc, xall, eall, up)
    return down.T, up, rms.reshape(())


def solution(mesh):
    in_specs = (
        P("dp", "head"),
        P("dp", None),
        P(),
        P("head", None, None),
        P("dp", "head", None),
        P("dp", None),
    )
    out_specs = (P("head", None), P("head", None, None), P())
    return jax.shard_map(
        per_device, mesh=mesh, in_specs=in_specs, out_specs=out_specs, check_vma=False
    )
```

```python
import functools
import math

import jax
import jax.numpy as jnp
from jax import lax
from jax.experimental import pallas as pl
from jax.experimental.pallas import tpu as pltpu
from jax.sharding import PartitionSpec as P

MESH = pl.DeviceIdType.MESH
bf16 = jnp.bfloat16
f32 = jnp.float32

D = 7168
TOKENS = 16384
LAT = 512
ROPE = 64
COLS = LAT + ROPE
DH2 = 256
NX, NZ, NY, NC = 4, 8, 4, 2
TOK = 512
HALF = TOK // NC
QUART = HALF // NY
DLOC = 896
XROWS = DLOC // NX
ZROWS = 32
UROWS = LAT // NX
AROWS, BROWS = 512, 384
AX, AZ = AROWS // NX, AROWS // (NX * NZ)
BZ = BROWS // NZ
UA, UB = 320, 192
UAX, UBX = UA // NX, UB // NX

VMEM_LIMIT = 40 * 1024 * 1024

coef_a = 3.4445
coef_b = -4.775
coef_c = 2.0315

BLOCK_ROWS = [128, 128, 128, 128, 64]
PACK = []
at = 0
for bi in range(5):
    for bj in range(bi, 5):
        PACK.append((bi, bj, at, BLOCK_ROWS[bi]))
        at += BLOCK_ROWS[bi]
PACKED = at
GHALF = PACKED // NC
GQUART = GHALF // NY


def dot(a, b):
    return lax.dot_general(a, b, (((1,), (0,)), ((), ())), preferred_element_type=f32)


def dot_nt(a, b):
    return lax.dot_general(a, b, (((1,), (1,)), ((), ())), preferred_element_type=f32)


def split(value):
    high = value.astype(bf16)
    low = (value - high.astype(f32)).astype(bf16)
    return high, low


def eye(rows, cols):
    row_id = lax.broadcasted_iota(jnp.int32, (rows, cols), 0)
    col_id = lax.broadcasted_iota(jnp.int32, (rows, cols), 1)
    return row_id == col_id


class Small:
    def prepare(self, value):
        return split(value[0])

    def product(self, a, b):
        return (dot(a[0], b[0]) + dot(a[0], b[1]) + dot(a[1], b[0]),)

    def rough(self, a, b):
        return (dot(a[0], b[0]),)


class Large:
    def prepare(self, value):
        main, corner = value
        rest = jnp.concatenate([main[LAT:, :].T, corner], axis=0)
        rest = split(rest)
        return split(main), rest, jnp.concatenate(rest, axis=1)

    def corner(self, a, b):
        (main_h, main_l), (rest_h, rest_l), _ = a
        left = jnp.concatenate([main_h[LAT:], main_l[LAT:]], axis=0)
        side = jnp.concatenate([rest_h[LAT:], rest_l[LAT:]], axis=0)
        out = dot(left, b[2][:LAT]) + dot(side, b[2][LAT:])
        return out[:ROPE, :ROPE] + out[:ROPE, ROPE:] + out[ROPE:, :ROPE]

    def product(self, a, b):
        (main_h, main_l), (rest_h, _), pair = a
        cols_h, cols_l = b[0]
        side = jnp.concatenate([pair, rest_h], axis=1)
        under = jnp.concatenate([cols_h[LAT:], cols_h[LAT:], cols_l[LAT:]], axis=0)

        def block(rows, cols):
            total = dot(main_h[rows], cols_h[:LAT, cols]) + dot(main_h[rows], cols_l[:LAT, cols])
            total += dot(main_l[rows], cols_h[:LAT, cols])
            return total + dot(side[rows], under[:, cols])

        left = block(slice(0, COLS), slice(0, DH2))
        right = block(slice(DH2, COLS), slice(DH2, LAT))
        right = jnp.concatenate([left[DH2:LAT].T, right], axis=0)
        return jnp.concatenate([left, right], axis=1), self.corner(a, b)

    def rough(self, a, b):
        main_h, rest_h = a[0][0], a[1][0]
        cols_h, tail_h = b[0][0], b[1][0]

        def block(rows, cols):
            return dot(main_h[rows], cols_h[:LAT, cols]) + dot(rest_h[rows], cols_h[LAT:, cols])

        left = block(slice(0, COLS), slice(0, DH2))
        right = block(slice(DH2, COLS), slice(DH2, LAT))
        right = jnp.concatenate([left[DH2:LAT].T, right], axis=0)
        corner = dot(main_h[LAT:], tail_h[:LAT]) + dot(rest_h[LAT:], tail_h[LAT:])
        return jnp.concatenate([left, right], axis=1), corner


class NewtonSchulz:
    def __init__(self, form, gram, mix):
        self.form, self.gram, self.mix = form, gram, mix

    def load(self, refs):
        return tuple(ref[...] for ref in refs)

    def store(self, refs, value):
        for ref, part in zip(refs, value):
            ref[...] = part

    def mixer(self, parts):
        square = self.form.product(parts, parts)
        out = []
        for ref, part in zip(self.gram, square):
            out.append(coef_b * ref[...] + coef_c * part + jnp.where(eye(*part.shape), coef_a, 0.0))
        return tuple(out)

    def advance(self, parts, mixed):
        half = self.form.prepare(self.form.product(parts, mixed))
        self.store(self.gram, self.form.product(half, mixed))

    def first(self):
        parts = self.form.prepare(self.load(self.gram))
        mixed = self.mixer(parts)
        self.store(self.mix, mixed)
        self.advance(parts, self.form.prepare(mixed))

    def middle(self, count, hook=lambda step: None):
        def body(step, carry):
            hook(step)
            parts = self.form.prepare(self.load(self.gram))
            mixed = self.form.prepare(self.mixer(parts))
            self.advance(parts, mixed)
            mix = self.form.prepare(self.load(self.mix))
            self.store(self.mix, self.form.rough(mix, mixed) if isinstance(self.form, Large) else self.form.product(mix, mixed))
            return carry

        lax.fori_loop(0, count, body, 0)

    def last(self):
        parts = self.form.prepare(self.load(self.gram))
        mixed = self.form.prepare(self.mixer(parts))
        mix = self.form.prepare(self.load(self.mix))
        return self.form.rough(mix, mixed)


def kernel(
    kv, w, acts, lat, gain, rope, up_out, rms_out, xall, eall, qm_out, qc_out,
    pcs, rcc, csum, ysend, yrecv, comp, acts_t, usend, uxr, uzs, uzr, vzr, vxs, vxr, u,
    dsend, axr, azs, azr, bzr, bxr, esend, exr, fsend, frecv, frows,
    gpk, gcr, gsum, gyr, gfull, a_main, a_corner, q_main, q_corner, ua_ref, uq_ref,
    s_c, r_c, s_yr, r_yr, s_ya, r_ya, s_ca, r_ca,
    s_ux, r_ux, s_uz, r_uz, s_vz, r_vz, s_vx, r_vx, s_ua, r_ua, s_ub, r_ub, s_oz, r_oz, s_ow, r_ow, s_ox, r_ox,
    s_ax, r_ax, s_az, r_az, s_bz, r_bz, s_bx, r_bx,
    s_gaz, r_gaz, s_gax, r_gax, s_gbz, r_gbz,
    s_ex, r_ex, s_ez, r_ez, s_fz, r_fz, s_fx, r_fx,
    s_gc, r_gc, s_gr, r_gr, s_ga, r_ga, s_gb, r_gb,
):
    dp = lax.axis_index("dp")
    hd = lax.axis_index("head")
    z, x = dp // NX, dp % NX
    y, c = hd // NC, hd % NC

    def to_x(j):
        return (z * NX + (x + j) % NX, hd)

    def to_z(j):
        return (((z + j) % NZ) * NX + x, hd)

    def to_y(j):
        return (dp, ((y + j) % NY) * NC + c)

    other = (dp, y * NC + (1 - c))
    started = []

    def send(src, dst, s, r, device):
        copy = pltpu.make_async_remote_copy(
            src_ref=src, dst_ref=dst, send_sem=s, recv_sem=r,
            device_id=device, device_id_type=MESH,
        )
        copy.start()
        started.append(copy)
        return copy

    def ds(start, size, unit=None):
        return pl.ds(pl.multiple_of(start, unit or size), size)

    def to_all_x(src, dst, s, r):
        return [send(src(j), dst(j), s.at[j - 1], r.at[j - 1], to_x(j)) for j in range(1, NX)]

    def to_all_z(src, dst, s, r):
        return [send(src(j), dst(j), s.at[j - 1], r.at[j - 1], to_z(j)) for j in range(1, NZ)]

    def received(copies, total, slots):
        for i, copy in enumerate(copies):
            copy.wait_recv()
            total += slots[i].astype(f32)
        return total

    barrier = pltpu.get_barrier_semaphore()
    peers = [other] + [to_y(j) for j in range(1, NY)]
    peers += [to_x(j) for j in range(1, NX)] + [to_z(j) for j in range(1, NZ)]
    for peer in peers:
        pl.semaphore_signal(barrier, inc=1, device_id=peer, device_id_type=MESH)

    def scatter_x(src, dst, s, r):
        return [
            send(src.at[ds(((x + j) % NX) * XROWS, XROWS)], dst.at[j - 1], s.at[j - 1], r.at[j - 1], to_x(j))
            for j in range(1, NX)
        ]

    def sum_x(copies, src, dst):
        for copy in copies:
            copy.wait_recv()
        part = src[ds(x * XROWS, XROWS), :].astype(f32)
        for j in range(NX - 1):
            part += dst[j].astype(f32)
        return part

    def scatter_z(part, src, dst, s, r):
        src[0:XROWS, :] = part.astype(bf16)
        src[XROWS : NZ * ZROWS, :] = jnp.zeros((NZ * ZROWS - XROWS, src.shape[1]), bf16)
        return [
            send(src.at[ds(((z + j) % NZ) * ZROWS, ZROWS)], dst.at[j - 1], s.at[j - 1], r.at[j - 1], to_z(j))
            for j in range(1, NZ)
        ]

    def sum_z(copies, src, dst):
        part = src[ds(z * ZROWS, ZROWS), :].astype(f32)
        for j in range(1, NZ):
            copies[j - 1].wait_recv()
            part += dst[j - 1].astype(f32)
        return part

    def gather_z(part, rows, s, r):
        rows[ds(z * ZROWS, ZROWS), :] = part.astype(bf16)
        mine = rows.at[ds(z * ZROWS, ZROWS)]
        return [send(mine, mine, s.at[j - 1], r.at[j - 1], to_z(j)) for j in range(1, NZ)]

    def gather_x(copies, rows, every, s, r):
        for copy in copies:
            copy.wait_recv()
        block = ds(x * XROWS, XROWS)
        out = [
            send(rows.at[pl.ds(0, XROWS)], every.at[block], s.at[j - 1], r.at[j - 1], to_x(j))
            for j in range(1, NX)
        ]
        every[block, :] = rows[0:XROWS, :]
        return out

    def cot_rows(start):
        rows = ds(start, HALF)
        total = dot_nt(kv[rows, 0:DH2], w[0])
        for h in range(1, 8):
            total += dot_nt(kv[rows, h * DH2 : (h + 1) * DH2], w[h])
        return total

    pcs[...] = cot_rows((1 - c) * HALF).astype(bf16)
    pl.semaphore_wait(barrier, len(peers))
    first = send(pcs, rcc, s_c, r_c, other)
    csum[...] = cot_rows(c * HALF)
    lat32 = lat[...].astype(f32)
    gain32 = gain[...].astype(f32).reshape(1, LAT)
    inv = lax.rsqrt(jnp.mean(lat32 * lat32, axis=1, keepdims=True) + 1e-06)
    normed_t = (lat32 * inv * gain32).astype(bf16).T
    for h in range(8):
        cols = slice(h * DH2, (h + 1) * DH2)
        usend[:, cols] = dot(normed_t, kv[:, cols]).astype(bf16)

    u_x = to_all_x(lambda j: usend.at[ds(((x + j) % NX) * UAX, UAX)], lambda j: uxr.at[j - 1], s_ux, r_ux)
    v_z = to_all_z(
        lambda j: usend.at[pl.ds(UA, UB), ds(((z + j) % NZ) * DH2, DH2)], lambda j: vzr.at[j - 1], s_vz, r_vz
    )
    acts_t[...] = acts[...].T
    esend[...] = jnp.concatenate(
        [dot_nt(acts_t[...], rope[...]).astype(bf16), jnp.zeros((DLOC, 128 - ROPE), bf16)], axis=1
    )
    e_x = scatter_x(esend, exr, s_ex, r_ex)
    first.wait_recv()
    csum[...] += rcc[...].astype(f32)
    ysend[...] = csum[...].astype(bf16)
    y_reduce = [
        send(ysend.at[ds(((y + j) % NY) * QUART, QUART)], yrecv.at[j - 1],
             s_yr.at[j - 1], r_yr.at[j - 1], to_y(j))
        for j in range(1, NY)
    ]
    e_z = scatter_z(sum_x(e_x, esend, exr), fsend, frecv, s_ez, r_ez)
    total = csum[ds(y * QUART, QUART), :]
    for j in range(1, NY):
        y_reduce[j - 1].wait_recv()
        total += yrecv[j - 1].astype(f32)
    own = c * HALF + y * QUART
    lat_q = lat[ds(own, QUART), :].astype(f32)
    inv_q = lax.rsqrt(jnp.mean(lat_q * lat_q, axis=1, keepdims=True) + 1e-06)
    scaled = total * gain32
    grad = inv_q * scaled - lat_q * inv_q**3 * jnp.mean(lat_q * scaled, axis=1, keepdims=True)
    comp[ds(own, QUART), :] = grad.astype(bf16)
    mine = comp.at[ds(own, QUART)]
    y_all = [send(mine, mine, s_ya.at[j - 1], r_ya.at[j - 1], to_y(j)) for j in range(1, NY)]
    c_all = [send(mine, mine, s_ca.at[0], r_ca.at[0], other)]
    e_az = gather_z(sum_z(e_z, fsend, frecv), frows, s_fz, r_fz)
    for j in range(1, NY):
        y_all[j - 1].wait_recv()
        piece = comp.at[ds(c * HALF + ((y - j + NY) % NY) * QUART, QUART)]
        c_all.append(send(piece, piece, s_ca.at[j], r_ca.at[j], other))
    for copy in c_all:
        copy.wait_recv()
    dsend[AROWS:, :] = dot(acts_t[AROWS:, :], comp[...]).astype(bf16)
    b_z = to_all_z(
        lambda j: dsend.at[ds(AROWS + ((z + j) % NZ) * BZ, BZ, 16)], lambda j: bzr.at[j - 1], s_bz, r_bz
    )
    dsend[0:AROWS, :] = dot(acts_t[0:AROWS, :], comp[...]).astype(bf16)
    a_x = to_all_x(lambda j: dsend.at[ds(((x + j) % NX) * AX, AX)], lambda j: axr.at[j - 1], s_ax, r_ax)
    e_ax = gather_x(e_az, frows, eall, s_fx, r_fx)
    part = received(v_z, usend[UA:, ds(z * DH2, DH2)].astype(f32), vzr)
    vxs[...] = part.astype(bf16)
    v_x = to_all_x(lambda j: vxs.at[ds(((x + j) % NX) * UBX, UBX)], lambda j: vxr.at[j - 1], s_vx, r_vx)
    azs[...] = received(a_x, dsend[ds(x * AX, AX), :].astype(f32), axr).astype(bf16)
    a_z = to_all_z(lambda j: azs.at[ds(((z + j) % NZ) * AZ, AZ)], lambda j: azr.at[j - 1], s_az, r_az)
    part = received(b_z, dsend[ds(AROWS + z * BZ, BZ, 16), :].astype(f32), bzr)
    bxr[x] = part.astype(bf16)
    mine_b = bxr.at[x]
    b_x = to_all_x(lambda j: mine_b, lambda j: mine_b, s_bx, r_bx)
    own = ds(x * AX + z * AZ, AZ)
    xall[own, :] = received(a_z, azs[ds(z * AZ, AZ), :].astype(f32), azr).astype(bf16)
    mine = xall.at[own]
    g_az = to_all_z(lambda j: mine, lambda j: mine, s_gaz, r_gaz)
    for copy in b_x:
        copy.wait_recv()
    part = bxr[0].astype(f32)
    for i in range(1, NX):
        part += bxr[i].astype(f32)
    own_z = ds(AROWS + z * BZ, BZ, 16)
    xall[own_z, :] = part.astype(bf16)
    mine_z = xall.at[own_z]
    g_bz = to_all_z(lambda j: mine_z, lambda j: mine_z, s_gbz, r_gbz)
    for copy in g_az:
        copy.wait_recv()
    mine_x = xall.at[ds(x * AX, AX)]
    g_ax = to_all_x(lambda j: mine_x, lambda j: mine_x, s_gax, r_gax)
    for copy in u_x:
        copy.wait_recv()
    for h in range(8):
        cols = slice(h * DH2, (h + 1) * DH2)
        part = usend[ds(x * UAX, UAX), cols].astype(f32)
        for j in range(NX - 1):
            part += uxr[j, :, cols].astype(f32)
        uzs[h] = part.astype(bf16)
    u_z = to_all_z(lambda j: uzs.at[(z + j) % NZ], lambda j: uzr.at[j - 1], s_uz, r_uz)
    for copy in g_ax + g_bz + e_ax:
        copy.wait_recv()
    main_t = [xall[:, i * 128 : (i + 1) * 128].T for i in range(4)]
    tail_t = eall[...].T
    for bi in range(5):
        size = BLOCK_ROWS[bi]
        lhs = main_t[bi] if bi < 4 else tail_t[0:size, :]
        tail = dot(lhs, eall[...])
        main = dot(lhs, xall[:, bi * 128 : LAT]) if bi < 4 else None
        for pi, pj, start, _ in PACK:
            if pi == bi:
                gpk[start : start + size, :] = tail if pj == 4 else main[:, (pj - bi) * 128 : (pj - bi + 1) * 128]
    g_c = send(gpk.at[ds((1 - c) * GHALF, GHALF)], gcr, s_gc, r_gc, other)
    g_c.wait_recv()
    gsum[...] = gpk[ds(c * GHALF, GHALF), :] + gcr[...]
    g_y = [
        send(gsum.at[ds(((y + j) % NY) * GQUART, GQUART)], gyr.at[j - 1],
             s_gr.at[j - 1], r_gr.at[j - 1], to_y(j))
        for j in range(1, NY)
    ]
    rows_a, rows_b = ds(x * UAX, UAX), ds(UA + x * UBX, UBX, 16)
    u[rows_b, :] = received(v_x, vxs[ds(x * UBX, UBX), :].astype(f32), vxr).astype(bf16)
    u_b = to_all_x(lambda j: u.at[rows_b], lambda j: u.at[rows_b], s_ub, r_ub)
    u[rows_a, :] = received(u_z, uzs[z].astype(f32), uzr).astype(bf16)
    u_a = to_all_x(lambda j: u.at[rows_a], lambda j: u.at[rows_a], s_ua, r_ua)
    for copy in u_a + u_b:
        copy.wait_recv()
    uval = u[...]
    ugram = dot(uval.T, uval)
    usq = jnp.sum(jnp.where(eye(DH2, DH2), ugram, 0.0), keepdims=True)
    unorm = 1.0 / (jnp.sqrt(usq) + 1e-07)
    ua_ref[...] = ugram * unorm * unorm
    up_steps = NewtonSchulz(Small(), (ua_ref,), (uq_ref,))
    up_steps.first()
    part = gsum[ds(y * GQUART, GQUART), :]
    for j in range(1, NY):
        g_y[j - 1].wait_recv()
        part += gyr[j - 1]
    own = c * GHALF + y * GQUART
    gfull[ds(own, GQUART), :] = part
    g_mine = gfull.at[ds(own, GQUART)]
    g_all = [send(g_mine, g_mine, s_ga.at[j - 1], r_ga.at[j - 1], to_y(j)) for j in range(1, NY)]
    g_fwd = [send(g_mine, g_mine, s_gb.at[0], r_gb.at[0], other)]
    up_steps.middle(3)
    uq = (up_steps.last()[0] * (unorm * (0.2 * math.sqrt(LAT)))).astype(bf16)
    near, far = ds(x * UROWS, UROWS), ds(((x + 2) % NX) * UROWS, UROWS)
    up_out[z, near, :] = dot(u[near, :], uq).astype(bf16)
    up_out[z, far, :] = dot(u[far, :], uq).astype(bf16)
    half = UROWS // 2
    parts = [ds(x * UROWS + i * half, half) for i in range(2)]
    o_z = []
    for i, rows in enumerate(parts):
        o_near = up_out.at[z, rows]
        o_z.append(to_all_z(lambda j: o_near, lambda j: o_near, s_oz.at[i], r_oz.at[i]))
    o_far = up_out.at[z, far]
    o_w = to_all_z(lambda j: o_far, lambda j: o_far, s_ow, r_ow)
    for j in range(1, NY):
        g_all[j - 1].wait_recv()
        piece = gfull.at[ds(c * GHALF + ((y - j + NY) % NY) * GQUART, GQUART)]
        g_fwd.append(send(piece, piece, s_gb.at[j], r_gb.at[j], other))
    for copy in g_fwd:
        copy.wait_recv()
    sq = jnp.zeros((1, 1), f32)
    for bi, bj, start, size in PACK:
        if bi == bj:
            block = gfull[start : start + size, :]
            sq += jnp.sum(jnp.where(eye(size, 128), block, 0.0), keepdims=True)
    norm = 1.0 / (jnp.sqrt(sq) + 1e-07)
    rms_out[0] = jnp.sqrt(sq / float(TOKENS * D * COLS))[0, 0]
    for bi, bj, start, size in PACK:
        block = gfull[start : start + size, :] * norm * norm
        rows = slice(bi * 128, bi * 128 + size)
        if bj < 4:
            a_main[rows, bj * 128 : (bj + 1) * 128] = block
        elif bi == 4:
            a_corner[...] = block[:, 0:ROPE]
        if bi != bj:
            wide = BLOCK_ROWS[bj]
            a_main[bj * 128 : bj * 128 + wide, rows] = block.T[0:wide, :]
    steps = NewtonSchulz(Large(), (a_main, a_corner), (q_main, q_corner))
    o_x = []
    for i, rows in enumerate(parts):
        o_rows = up_out.at[:, rows]
        o_x.append([
            pltpu.make_async_remote_copy(
                src_ref=o_rows, dst_ref=o_rows, send_sem=s_ox.at[i, k], recv_sem=r_ox.at[i, k],
                device_id=to_x(j), device_id_type=MESH,
            )
            for k, j in enumerate((1, 3))
        ])

    def pass_on(i):
        for copy in o_z[i]:
            copy.wait_recv()
        for copy in o_x[i]:
            copy.start()

    pass_on(0)
    steps.first()
    steps.middle(3, lambda step: pl.when(step == 1)(lambda: pass_on(1)))
    main, corner = steps.last()
    scale = norm * (0.2 * math.sqrt(D))
    qm_out[...] = (main * scale).astype(bf16)
    qc_out[...] = (corner * scale).astype(bf16)
    for copy in o_w + o_x[0] + o_x[1]:
        copy.wait_recv()
    for copy in started + o_x[0] + o_x[1]:
        copy.wait_send()


def finish(qm, qc, xall, eall, up, down_out, up_out, sem):
    store = pltpu.make_async_copy(up, up_out, sem)
    store.start()
    tail = eall[:, 0:ROPE]
    side = qm[LAT:, :].T
    down_out[0:LAT, :] = (dot_nt(qm[0:LAT, :], xall[...]) + dot_nt(side, tail)).astype(bf16)
    down_out[LAT:, :] = (dot_nt(qm[LAT:, :], xall[...]) + dot_nt(qc[...], tail)).astype(bf16)
    store.wait()


def per_device(acts, latent, kv_gain, up_weight, kv_cot, rope_grad):
    vmem = pltpu.VMEM
    one = pltpu.SemaphoreType.DMA
    sems = lambda *n: [pltpu.SemaphoreType.DMA(n), pltpu.SemaphoreType.DMA(n)]

    scratch = [
        vmem((HALF, LAT), bf16), vmem((HALF, LAT), bf16), vmem((HALF, LAT), f32),
        vmem((HALF, LAT), bf16), vmem((3, QUART, LAT), bf16), vmem((TOK, LAT), bf16),
        vmem((DLOC, TOK), bf16),
        vmem((LAT, 8 * DH2), bf16), vmem((3, UAX, 8 * DH2), bf16), vmem((8, UAX, DH2), bf16),
        vmem((7, UAX, DH2), bf16), vmem((7, UB, DH2), bf16), vmem((UB, DH2), bf16),
        vmem((3, UBX, DH2), bf16), vmem((LAT, DH2), bf16),
        vmem((DLOC, LAT), bf16), vmem((3, AX, LAT), bf16), vmem((AX, LAT), bf16), vmem((7, AZ, LAT), bf16),
        vmem((7, BZ, LAT), bf16), vmem((NX, BZ, LAT), bf16),
        vmem((DLOC, 128), bf16), vmem((3, XROWS, 128), bf16), vmem((NZ * ZROWS, 128), bf16),
        vmem((7, ZROWS, 128), bf16), vmem((NZ * ZROWS, 128), bf16),
        vmem((PACKED, 128), f32), vmem((GHALF, 128), f32), vmem((GHALF, 128), f32),
        vmem((3, GQUART, 128), f32), vmem((PACKED, 128), f32),
        vmem((COLS, LAT), f32), vmem((ROPE, ROPE), f32), vmem((COLS, LAT), f32), vmem((ROPE, ROPE), f32),
        vmem((DH2, DH2), f32), vmem((DH2, DH2), f32),
    ]
    scratch += [one, one] + sems(3) + sems(3) + sems(4)
    scratch += sems(3) + sems(7) + sems(7) + sems(3) + sems(3) + sems(3) + sems(2, 7) + sems(7) + sems(2, 2)
    scratch += sems(3) + sems(7) + sems(7) + sems(3) + sems(7) + sems(3) + sems(7)
    scratch += sems(3) + sems(7) + sems(7) + sems(3)
    scratch += [one, one] + sems(3) + sems(3) + sems(4)
    in_vmem = pl.BlockSpec(memory_space=pltpu.VMEM)
    shape = jax.ShapeDtypeStruct
    up, rms, xall, eall, qm, qc = pl.pallas_call(
        kernel,
        out_shape=(
            shape((8, LAT, DH2), bf16), shape((1,), f32), shape((DLOC, LAT), bf16), shape((DLOC, 128), bf16),
            shape((COLS, LAT), bf16), shape((ROPE, ROPE), bf16),
        ),
        in_specs=[in_vmem] * 6,
        out_specs=(in_vmem, pl.BlockSpec(memory_space=pltpu.SMEM), in_vmem, in_vmem, in_vmem, in_vmem),
        scratch_shapes=scratch,
        name="muon",
        compiler_params=pltpu.CompilerParams(
            collective_id=0, has_side_effects=True, vmem_limit_bytes=VMEM_LIMIT
        ),
    )(kv_cot.reshape(TOK, 8 * DH2), up_weight, acts, latent, kv_gain, rope_grad.T)
    down, up = pl.pallas_call(
        finish,
        out_shape=(shape((COLS, DLOC), bf16), shape((8, LAT, DH2), bf16)),
        in_specs=[in_vmem] * 5,
        out_specs=(in_vmem, pl.BlockSpec(memory_space=pl.ANY)),
        scratch_shapes=[one],
        name="finish",
        compiler_params=pltpu.CompilerParams(vmem_limit_bytes=VMEM_LIMIT),
    )(qm, qc, xall, eall, up)
    return down.T, up, rms.reshape(())


def solution(mesh):
    in_specs = (
        P("dp", "head"),
        P("dp", None),
        P(),
        P("head", None, None),
        P("dp", "head", None),
        P("dp", None),
    )
    out_specs = (P("head", None), P("head", None, None), P())
    return jax.shard_map(
        per_device, mesh=mesh, in_specs=in_specs, out_specs=out_specs, check_vma=False
    )
```

```python
import functools
import math

import jax
import jax.numpy as jnp
from jax import lax
from jax.experimental import pallas as pl
from jax.experimental.pallas import tpu as pltpu
from jax.sharding import PartitionSpec as P

MESH = pl.DeviceIdType.MESH
bf16 = jnp.bfloat16
f32 = jnp.float32

D = 7168
TOKENS = 16384
LAT = 512
ROPE = 64
COLS = LAT + ROPE
DH2 = 256
NX, NZ, NY, NC = 4, 8, 4, 2
TOK = 512
HALF = TOK // NC
QUART = HALF // NY
DLOC = 896
XROWS = DLOC // NX
ZROWS = 32
UROWS = LAT // NX
AROWS, BROWS = 512, 384
AX, AZ = AROWS // NX, AROWS // (NX * NZ)
BZ = BROWS // NZ
UA, UB = 320, 192
UAX, UBX = UA // NX, UB // NX

VMEM_LIMIT = 40 * 1024 * 1024

coef_a = 3.4445
coef_b = -4.775
coef_c = 2.0315

BLOCK_ROWS = [128, 128, 128, 128, 64]
PACK = []
at = 0
for bi in range(5):
    for bj in range(bi, 5):
        PACK.append((bi, bj, at, BLOCK_ROWS[bi]))
        at += BLOCK_ROWS[bi]
PACKED = at
GHALF = PACKED // NC
GQUART = GHALF // NY


def dot(a, b):
    return lax.dot_general(a, b, (((1,), (0,)), ((), ())), preferred_element_type=f32)


def dot_nt(a, b):
    return lax.dot_general(a, b, (((1,), (1,)), ((), ())), preferred_element_type=f32)


def split(value):
    high = value.astype(bf16)
    low = (value - high.astype(f32)).astype(bf16)
    return high, low


def eye(rows, cols):
    row_id = lax.broadcasted_iota(jnp.int32, (rows, cols), 0)
    col_id = lax.broadcasted_iota(jnp.int32, (rows, cols), 1)
    return row_id == col_id


class Small:
    def prepare(self, value):
        return split(value[0])

    def product(self, a, b):
        return (dot(a[0], b[0]) + dot(a[0], b[1]) + dot(a[1], b[0]),)

    def rough(self, a, b):
        return (dot(a[0], b[0]),)


class Large:
    def prepare(self, value):
        main, corner = value
        rest = jnp.concatenate([main[LAT:, :].T, corner], axis=0)
        rest = split(rest)
        return split(main), rest, jnp.concatenate(rest, axis=1)

    def corner(self, a, b):
        (main_h, main_l), (rest_h, rest_l), _ = a
        left = jnp.concatenate([main_h[LAT:], main_l[LAT:]], axis=0)
        side = jnp.concatenate([rest_h[LAT:], rest_l[LAT:]], axis=0)
        out = dot(left, b[2][:LAT]) + dot(side, b[2][LAT:])
        return out[:ROPE, :ROPE] + out[:ROPE, ROPE:] + out[ROPE:, :ROPE]

    def product(self, a, b):
        (main_h, main_l), (rest_h, _), pair = a
        cols_h, cols_l = b[0]
        side = jnp.concatenate([pair, rest_h], axis=1)
        under = jnp.concatenate([cols_h[LAT:], cols_h[LAT:], cols_l[LAT:]], axis=0)

        def block(rows, cols):
            total = dot(main_h[rows], cols_h[:LAT, cols]) + dot(main_h[rows], cols_l[:LAT, cols])
            total += dot(main_l[rows], cols_h[:LAT, cols])
            return total + dot(side[rows], under[:, cols])

        left = block(slice(0, COLS), slice(0, DH2))
        right = block(slice(DH2, COLS), slice(DH2, LAT))
        right = jnp.concatenate([left[DH2:LAT].T, right], axis=0)
        return jnp.concatenate([left, right], axis=1), self.corner(a, b)

    def rough(self, a, b):
        main_h, rest_h = a[0][0], a[1][0]
        cols_h, tail_h = b[0][0], b[1][0]

        def block(rows, cols):
            return dot(main_h[rows], cols_h[:LAT, cols]) + dot(rest_h[rows], cols_h[LAT:, cols])

        left = block(slice(0, COLS), slice(0, DH2))
        right = block(slice(DH2, COLS), slice(DH2, LAT))
        right = jnp.concatenate([left[DH2:LAT].T, right], axis=0)
        corner = dot(main_h[LAT:], tail_h[:LAT]) + dot(rest_h[LAT:], tail_h[LAT:])
        return jnp.concatenate([left, right], axis=1), corner


class NewtonSchulz:
    def __init__(self, form, gram, mix):
        self.form, self.gram, self.mix = form, gram, mix

    def load(self, refs):
        return tuple(ref[...] for ref in refs)

    def store(self, refs, value):
        for ref, part in zip(refs, value):
            ref[...] = part

    def mixer(self, parts):
        square = self.form.product(parts, parts)
        out = []
        for ref, part in zip(self.gram, square):
            out.append(coef_b * ref[...] + coef_c * part + jnp.where(eye(*part.shape), coef_a, 0.0))
        return tuple(out)

    def advance(self, parts, mixed):
        half = self.form.prepare(self.form.product(parts, mixed))
        self.store(self.gram, self.form.product(half, mixed))

    def first(self):
        parts = self.form.prepare(self.load(self.gram))
        mixed = self.mixer(parts)
        self.store(self.mix, mixed)
        self.advance(parts, self.form.prepare(mixed))

    def middle(self, count, hook=lambda step: None):
        def body(step, carry):
            hook(step)
            parts = self.form.prepare(self.load(self.gram))
            mixed = self.form.prepare(self.mixer(parts))
            self.advance(parts, mixed)
            mix = self.form.prepare(self.load(self.mix))
            self.store(self.mix, self.form.rough(mix, mixed) if isinstance(self.form, Large) else self.form.product(mix, mixed))
            return carry

        lax.fori_loop(0, count, body, 0)

    def last(self):
        parts = self.form.prepare(self.load(self.gram))
        mixed = self.form.prepare(self.mixer(parts))
        mix = self.form.prepare(self.load(self.mix))
        return self.form.rough(mix, mixed)


def kernel(
    kv, w, acts, lat, gain, rope, up_out, rms_out, xall, eall, qm_out, qc_out,
    pcs, rcc, csum, ysend, yrecv, comp, acts_t, usend, uxr, uzs, uzr, vzr, vxs, vxr, u,
    dsend, axr, azs, azr, bzr, bxr, esend, exr, fsend, frecv, frows,
    gpk, gcr, gsum, gyr, gfull, a_main, a_corner, q_main, q_corner, ua_ref, uq_ref,
    s_c, r_c, s_yr, r_yr, s_ya, r_ya, s_ca, r_ca,
    s_ux, r_ux, s_uz, r_uz, s_vz, r_vz, s_vx, r_vx, s_ua, r_ua, s_ub, r_ub, s_oz, r_oz, s_ow, r_ow, s_ox, r_ox,
    s_ax, r_ax, s_az, r_az, s_bz, r_bz, s_bx, r_bx,
    s_gaz, r_gaz, s_gax, r_gax, s_gbz, r_gbz,
    s_ex, r_ex, s_ez, r_ez, s_fz, r_fz, s_fx, r_fx,
    s_gc, r_gc, s_gr, r_gr, s_ga, r_ga, s_gb, r_gb,
):
    dp = lax.axis_index("dp")
    hd = lax.axis_index("head")
    z, x = dp // NX, dp % NX
    y, c = hd // NC, hd % NC

    def to_x(j):
        return (z * NX + (x + j) % NX, hd)

    def to_z(j):
        return (((z + j) % NZ) * NX + x, hd)

    def to_y(j):
        return (dp, ((y + j) % NY) * NC + c)

    other = (dp, y * NC + (1 - c))
    started = []

    def send(src, dst, s, r, device):
        copy = pltpu.make_async_remote_copy(
            src_ref=src, dst_ref=dst, send_sem=s, recv_sem=r,
            device_id=device, device_id_type=MESH,
        )
        copy.start()
        started.append(copy)
        return copy

    def ds(start, size, unit=None):
        return pl.ds(pl.multiple_of(start, unit or size), size)

    def to_all_x(src, dst, s, r):
        return [send(src(j), dst(j), s.at[j - 1], r.at[j - 1], to_x(j)) for j in range(1, NX)]

    def to_all_z(src, dst, s, r):
        return [send(src(j), dst(j), s.at[j - 1], r.at[j - 1], to_z(j)) for j in range(1, NZ)]

    def received(copies, total, slots):
        for i, copy in enumerate(copies):
            copy.wait_recv()
            total += slots[i].astype(f32)
        return total

    barrier = pltpu.get_barrier_semaphore()
    peers = [other] + [to_y(j) for j in range(1, NY)]
    peers += [to_x(j) for j in range(1, NX)] + [to_z(j) for j in range(1, NZ)]
    for peer in peers:
        pl.semaphore_signal(barrier, inc=1, device_id=peer, device_id_type=MESH)

    def scatter_x(src, dst, s, r):
        return [
            send(src.at[ds(((x + j) % NX) * XROWS, XROWS)], dst.at[j - 1], s.at[j - 1], r.at[j - 1], to_x(j))
            for j in range(1, NX)
        ]

    def sum_x(copies, src, dst):
        for copy in copies:
            copy.wait_recv()
        part = src[ds(x * XROWS, XROWS), :].astype(f32)
        for j in range(NX - 1):
            part += dst[j].astype(f32)
        return part

    def scatter_z(part, src, dst, s, r):
        src[0:XROWS, :] = part.astype(bf16)
        src[XROWS : NZ * ZROWS, :] = jnp.zeros((NZ * ZROWS - XROWS, src.shape[1]), bf16)
        return [
            send(src.at[ds(((z + j) % NZ) * ZROWS, ZROWS)], dst.at[j - 1], s.at[j - 1], r.at[j - 1], to_z(j))
            for j in range(1, NZ)
        ]

    def sum_z(copies, src, dst):
        part = src[ds(z * ZROWS, ZROWS), :].astype(f32)
        for j in range(1, NZ):
            copies[j - 1].wait_recv()
            part += dst[j - 1].astype(f32)
        return part

    def gather_z(part, rows, s, r):
        rows[ds(z * ZROWS, ZROWS), :] = part.astype(bf16)
        mine = rows.at[ds(z * ZROWS, ZROWS)]
        return [send(mine, mine, s.at[j - 1], r.at[j - 1], to_z(j)) for j in range(1, NZ)]

    def gather_x(copies, rows, every, s, r):
        for copy in copies:
            copy.wait_recv()
        block = ds(x * XROWS, XROWS)
        out = [
            send(rows.at[pl.ds(0, XROWS)], every.at[block], s.at[j - 1], r.at[j - 1], to_x(j))
            for j in range(1, NX)
        ]
        every[block, :] = rows[0:XROWS, :]
        return out

    def cot_rows(start):
        rows = ds(start, HALF)
        total = dot_nt(kv[rows, 0:DH2], w[0])
        for h in range(1, 8):
            total += dot_nt(kv[rows, h * DH2 : (h + 1) * DH2], w[h])
        return total

    pcs[...] = cot_rows((1 - c) * HALF).astype(bf16)
    pl.semaphore_wait(barrier, len(peers))
    first = send(pcs, rcc, s_c, r_c, other)
    csum[...] = cot_rows(c * HALF)
    lat32 = lat[...].astype(f32)
    gain32 = gain[...].astype(f32).reshape(1, LAT)
    inv = lax.rsqrt(jnp.mean(lat32 * lat32, axis=1, keepdims=True) + 1e-06)
    normed_t = (lat32 * inv * gain32).astype(bf16).T
    for h in range(8):
        cols = slice(h * DH2, (h + 1) * DH2)
        usend[:, cols] = dot(normed_t, kv[:, cols]).astype(bf16)

    u_x = to_all_x(lambda j: usend.at[ds(((x + j) % NX) * UAX, UAX)], lambda j: uxr.at[j - 1], s_ux, r_ux)
    v_z = to_all_z(
        lambda j: usend.at[pl.ds(UA, UB), ds(((z + j) % NZ) * DH2, DH2)], lambda j: vzr.at[j - 1], s_vz, r_vz
    )
    acts_t[...] = acts[...].T
    esend[...] = jnp.concatenate(
        [dot_nt(acts_t[...], rope[...]).astype(bf16), jnp.zeros((DLOC, 128 - ROPE), bf16)], axis=1
    )
    e_x = scatter_x(esend, exr, s_ex, r_ex)
    first.wait_recv()
    csum[...] += rcc[...].astype(f32)
    ysend[...] = csum[...].astype(bf16)
    y_reduce = [
        send(ysend.at[ds(((y + j) % NY) * QUART, QUART)], yrecv.at[j - 1],
             s_yr.at[j - 1], r_yr.at[j - 1], to_y(j))
        for j in range(1, NY)
    ]
    e_z = scatter_z(sum_x(e_x, esend, exr), fsend, frecv, s_ez, r_ez)
    total = csum[ds(y * QUART, QUART), :]
    for j in range(1, NY):
        y_reduce[j - 1].wait_recv()
        total += yrecv[j - 1].astype(f32)
    own = c * HALF + y * QUART
    lat_q = lat[ds(own, QUART), :].astype(f32)
    inv_q = lax.rsqrt(jnp.mean(lat_q * lat_q, axis=1, keepdims=True) + 1e-06)
    scaled = total * gain32
    grad = inv_q * scaled - lat_q * inv_q**3 * jnp.mean(lat_q * scaled, axis=1, keepdims=True)
    comp[ds(own, QUART), :] = grad.astype(bf16)
    mine = comp.at[ds(own, QUART)]
    y_all = [send(mine, mine, s_ya.at[j - 1], r_ya.at[j - 1], to_y(j)) for j in range(1, NY)]
    c_all = [send(mine, mine, s_ca.at[0], r_ca.at[0], other)]
    e_az = gather_z(sum_z(e_z, fsend, frecv), frows, s_fz, r_fz)
    for j in range(1, NY):
        y_all[j - 1].wait_recv()
        piece = comp.at[ds(c * HALF + ((y - j + NY) % NY) * QUART, QUART)]
        c_all.append(send(piece, piece, s_ca.at[j], r_ca.at[j], other))
    for copy in c_all:
        copy.wait_recv()
    dsend[AROWS:, :] = dot(acts_t[AROWS:, :], comp[...]).astype(bf16)
    b_z = to_all_z(
        lambda j: dsend.at[ds(AROWS + ((z + j) % NZ) * BZ, BZ, 16)], lambda j: bzr.at[j - 1], s_bz, r_bz
    )
    dsend[0:AROWS, :] = dot(acts_t[0:AROWS, :], comp[...]).astype(bf16)
    a_x = to_all_x(lambda j: dsend.at[ds(((x + j) % NX) * AX, AX)], lambda j: axr.at[j - 1], s_ax, r_ax)
    e_ax = gather_x(e_az, frows, eall, s_fx, r_fx)
    part = received(v_z, usend[UA:, ds(z * DH2, DH2)].astype(f32), vzr)
    vxs[...] = part.astype(bf16)
    v_x = to_all_x(lambda j: vxs.at[ds(((x + j) % NX) * UBX, UBX)], lambda j: vxr.at[j - 1], s_vx, r_vx)
    azs[...] = received(a_x, dsend[ds(x * AX, AX), :].astype(f32), axr).astype(bf16)
    a_z = to_all_z(lambda j: azs.at[ds(((z + j) % NZ) * AZ, AZ)], lambda j: azr.at[j - 1], s_az, r_az)
    part = received(b_z, dsend[ds(AROWS + z * BZ, BZ, 16), :].astype(f32), bzr)
    bxr[x] = part.astype(bf16)
    mine_b = bxr.at[x]
    b_x = to_all_x(lambda j: mine_b, lambda j: mine_b, s_bx, r_bx)
    own = ds(x * AX + z * AZ, AZ)
    xall[own, :] = received(a_z, azs[ds(z * AZ, AZ), :].astype(f32), azr).astype(bf16)
    mine = xall.at[own]
    g_az = to_all_z(lambda j: mine, lambda j: mine, s_gaz, r_gaz)
    for copy in b_x:
        copy.wait_recv()
    part = bxr[0].astype(f32)
    for i in range(1, NX):
        part += bxr[i].astype(f32)
    own_z = ds(AROWS + z * BZ, BZ, 16)
    xall[own_z, :] = part.astype(bf16)
    mine_z = xall.at[own_z]
    g_bz = to_all_z(lambda j: mine_z, lambda j: mine_z, s_gbz, r_gbz)
    for copy in g_az:
        copy.wait_recv()
    mine_x = xall.at[ds(x * AX, AX)]
    g_ax = to_all_x(lambda j: mine_x, lambda j: mine_x, s_gax, r_gax)
    for copy in u_x:
        copy.wait_recv()
    for h in range(8):
        cols = slice(h * DH2, (h + 1) * DH2)
        part = usend[ds(x * UAX, UAX), cols].astype(f32)
        for j in range(NX - 1):
            part += uxr[j, :, cols].astype(f32)
        uzs[h] = part.astype(bf16)
    u_z = to_all_z(lambda j: uzs.at[(z + j) % NZ], lambda j: uzr.at[j - 1], s_uz, r_uz)
    for copy in g_ax + g_bz + e_ax:
        copy.wait_recv()
    main_t = [xall[:, i * 128 : (i + 1) * 128].T for i in range(4)]
    tail_t = eall[...].T
    for bi in range(5):
        size = BLOCK_ROWS[bi]
        lhs = main_t[bi] if bi < 4 else tail_t[0:size, :]
        tail = dot(lhs, eall[...])
        main = dot(lhs, xall[:, bi * 128 : LAT]) if bi < 4 else None
        for pi, pj, start, _ in PACK:
            if pi == bi:
                gpk[start : start + size, :] = tail if pj == 4 else main[:, (pj - bi) * 128 : (pj - bi + 1) * 128]
    g_c = send(gpk.at[ds((1 - c) * GHALF, GHALF)], gcr, s_gc, r_gc, other)
    g_c.wait_recv()
    gsum[...] = gpk[ds(c * GHALF, GHALF), :] + gcr[...]
    g_y = [
        send(gsum.at[ds(((y + j) % NY) * GQUART, GQUART)], gyr.at[j - 1],
             s_gr.at[j - 1], r_gr.at[j - 1], to_y(j))
        for j in range(1, NY)
    ]
    rows_a, rows_b = ds(x * UAX, UAX), ds(UA + x * UBX, UBX, 16)
    u[rows_b, :] = received(v_x, vxs[ds(x * UBX, UBX), :].astype(f32), vxr).astype(bf16)
    u_b = to_all_x(lambda j: u.at[rows_b], lambda j: u.at[rows_b], s_ub, r_ub)
    u[rows_a, :] = received(u_z, uzs[z].astype(f32), uzr).astype(bf16)
    u_a = to_all_x(lambda j: u.at[rows_a], lambda j: u.at[rows_a], s_ua, r_ua)
    for copy in u_a + u_b:
        copy.wait_recv()
    uval = u[...]
    ugram = dot(uval.T, uval)
    usq = jnp.sum(jnp.where(eye(DH2, DH2), ugram, 0.0), keepdims=True)
    unorm = 1.0 / (jnp.sqrt(usq) + 1e-07)
    ua_ref[...] = ugram * unorm * unorm
    up_steps = NewtonSchulz(Small(), (ua_ref,), (uq_ref,))
    up_steps.first()
    part = gsum[ds(y * GQUART, GQUART), :]
    for j in range(1, NY):
        g_y[j - 1].wait_recv()
        part += gyr[j - 1]
    own = c * GHALF + y * GQUART
    gfull[ds(own, GQUART), :] = part
    g_mine = gfull.at[ds(own, GQUART)]
    g_all = [send(g_mine, g_mine, s_ga.at[j - 1], r_ga.at[j - 1], to_y(j)) for j in range(1, NY)]
    g_fwd = [send(g_mine, g_mine, s_gb.at[0], r_gb.at[0], other)]
    up_steps.middle(3)
    uq = (up_steps.last()[0] * (unorm * (0.2 * math.sqrt(LAT)))).astype(bf16)
    near, far = ds(x * UROWS, UROWS), ds(((x + 2) % NX) * UROWS, UROWS)
    up_out[z, near, :] = dot(u[near, :], uq).astype(bf16)
    up_out[z, far, :] = dot(u[far, :], uq).astype(bf16)
    half = UROWS // 2
    parts = [ds(x * UROWS + i * half, half) for i in range(2)]
    o_z = []
    for i, rows in enumerate(parts):
        o_near = up_out.at[z, rows]
        o_z.append(to_all_z(lambda j: o_near, lambda j: o_near, s_oz.at[i], r_oz.at[i]))
    o_far = up_out.at[z, far]
    o_w = to_all_z(lambda j: o_far, lambda j: o_far, s_ow, r_ow)
    for j in range(1, NY):
        g_all[j - 1].wait_recv()
        piece = gfull.at[ds(c * GHALF + ((y - j + NY) % NY) * GQUART, GQUART)]
        g_fwd.append(send(piece, piece, s_gb.at[j], r_gb.at[j], other))
    for copy in g_fwd:
        copy.wait_recv()
    sq = jnp.zeros((1, 1), f32)
    for bi, bj, start, size in PACK:
        if bi == bj:
            block = gfull[start : start + size, :]
            sq += jnp.sum(jnp.where(eye(size, 128), block, 0.0), keepdims=True)
    norm = 1.0 / (jnp.sqrt(sq) + 1e-07)
    rms_out[0] = jnp.sqrt(sq / float(TOKENS * D * COLS))[0, 0]
    for bi, bj, start, size in PACK:
        block = gfull[start : start + size, :] * norm * norm
        rows = slice(bi * 128, bi * 128 + size)
        if bj < 4:
            a_main[rows, bj * 128 : (bj + 1) * 128] = block
        elif bi == 4:
            a_corner[...] = block[:, 0:ROPE]
        if bi != bj:
            wide = BLOCK_ROWS[bj]
            a_main[bj * 128 : bj * 128 + wide, rows] = block.T[0:wide, :]
    steps = NewtonSchulz(Large(), (a_main, a_corner), (q_main, q_corner))
    o_x = []
    for i, rows in enumerate(parts):
        o_rows = up_out.at[:, rows]
        o_x.append([
            pltpu.make_async_remote_copy(
                src_ref=o_rows, dst_ref=o_rows, send_sem=s_ox.at[i, k], recv_sem=r_ox.at[i, k],
                device_id=to_x(j), device_id_type=MESH,
            )
            for k, j in enumerate((1, 3))
        ])

    def pass_on(i):
        for copy in o_z[i]:
            copy.wait_recv()
        for copy in o_x[i]:
            copy.start()

    pass_on(0)
    steps.first()
    steps.middle(3, lambda step: pl.when(step == 2)(lambda: pass_on(1)))
    main, corner = steps.last()
    scale = norm * (0.2 * math.sqrt(D))
    qm_out[...] = (main * scale).astype(bf16)
    qc_out[...] = (corner * scale).astype(bf16)
    for copy in o_w + o_x[0] + o_x[1]:
        copy.wait_recv()
    for copy in started + o_x[0] + o_x[1]:
        copy.wait_send()


def finish(qm, qc, xall, eall, up, down_out, up_out, sem):
    store = pltpu.make_async_copy(up, up_out, sem)
    store.start()
    tail = eall[:, 0:ROPE]
    side = qm[LAT:, :].T
    down_out[0:LAT, :] = (dot_nt(qm[0:LAT, :], xall[...]) + dot_nt(side, tail)).astype(bf16)
    down_out[LAT:, :] = (dot_nt(qm[LAT:, :], xall[...]) + dot_nt(qc[...], tail)).astype(bf16)
    store.wait()


def per_device(acts, latent, kv_gain, up_weight, kv_cot, rope_grad):
    vmem = pltpu.VMEM
    one = pltpu.SemaphoreType.DMA
    sems = lambda *n: [pltpu.SemaphoreType.DMA(n), pltpu.SemaphoreType.DMA(n)]

    scratch = [
        vmem((HALF, LAT), bf16), vmem((HALF, LAT), bf16), vmem((HALF, LAT), f32),
        vmem((HALF, LAT), bf16), vmem((3, QUART, LAT), bf16), vmem((TOK, LAT), bf16),
        vmem((DLOC, TOK), bf16),
        vmem((LAT, 8 * DH2), bf16), vmem((3, UAX, 8 * DH2), bf16), vmem((8, UAX, DH2), bf16),
        vmem((7, UAX, DH2), bf16), vmem((7, UB, DH2), bf16), vmem((UB, DH2), bf16),
        vmem((3, UBX, DH2), bf16), vmem((LAT, DH2), bf16),
        vmem((DLOC, LAT), bf16), vmem((3, AX, LAT), bf16), vmem((AX, LAT), bf16), vmem((7, AZ, LAT), bf16),
        vmem((7, BZ, LAT), bf16), vmem((NX, BZ, LAT), bf16),
        vmem((DLOC, 128), bf16), vmem((3, XROWS, 128), bf16), vmem((NZ * ZROWS, 128), bf16),
        vmem((7, ZROWS, 128), bf16), vmem((NZ * ZROWS, 128), bf16),
        vmem((PACKED, 128), f32), vmem((GHALF, 128), f32), vmem((GHALF, 128), f32),
        vmem((3, GQUART, 128), f32), vmem((PACKED, 128), f32),
        vmem((COLS, LAT), f32), vmem((ROPE, ROPE), f32), vmem((COLS, LAT), f32), vmem((ROPE, ROPE), f32),
        vmem((DH2, DH2), f32), vmem((DH2, DH2), f32),
    ]
    scratch += [one, one] + sems(3) + sems(3) + sems(4)
    scratch += sems(3) + sems(7) + sems(7) + sems(3) + sems(3) + sems(3) + sems(2, 7) + sems(7) + sems(2, 2)
    scratch += sems(3) + sems(7) + sems(7) + sems(3) + sems(7) + sems(3) + sems(7)
    scratch += sems(3) + sems(7) + sems(7) + sems(3)
    scratch += [one, one] + sems(3) + sems(3) + sems(4)
    in_vmem = pl.BlockSpec(memory_space=pltpu.VMEM)
    shape = jax.ShapeDtypeStruct
    up, rms, xall, eall, qm, qc = pl.pallas_call(
        kernel,
        out_shape=(
            shape((8, LAT, DH2), bf16), shape((1,), f32), shape((DLOC, LAT), bf16), shape((DLOC, 128), bf16),
            shape((COLS, LAT), bf16), shape((ROPE, ROPE), bf16),
        ),
        in_specs=[in_vmem] * 6,
        out_specs=(in_vmem, pl.BlockSpec(memory_space=pltpu.SMEM), in_vmem, in_vmem, in_vmem, in_vmem),
        scratch_shapes=scratch,
        name="muon",
        compiler_params=pltpu.CompilerParams(
            collective_id=0, has_side_effects=True, vmem_limit_bytes=VMEM_LIMIT
        ),
    )(kv_cot.reshape(TOK, 8 * DH2), up_weight, acts, latent, kv_gain, rope_grad.T)
    down, up = pl.pallas_call(
        finish,
        out_shape=(shape((COLS, DLOC), bf16), shape((8, LAT, DH2), bf16)),
        in_specs=[in_vmem] * 5,
        out_specs=(in_vmem, pl.BlockSpec(memory_space=pl.ANY)),
        scratch_shapes=[one],
        name="finish",
        compiler_params=pltpu.CompilerParams(vmem_limit_bytes=VMEM_LIMIT),
    )(qm, qc, xall, eall, up)
    return down.T, up, rms.reshape(())


def solution(mesh):
    in_specs = (
        P("dp", "head"),
        P("dp", None),
        P(),
        P("head", None, None),
        P("dp", "head", None),
        P("dp", None),
    )
    out_specs = (P("head", None), P("head", None, None), P())
    return jax.shard_map(
        per_device, mesh=mesh, in_specs=in_specs, out_specs=out_specs, check_vma=False
    )
```
